256 devices in a mesh: dp: 16 (over x, y), seq: 16 (over z, core).
Axes of the slice: x: 4, y: 4, z: 8, core: 2. Of those that a mesh axis runs over, the one named last changes fastest.
Arguments:
- tokens: bfloat16 [49152, 4096], P(('dp', 'seq')), parts along dimension 0, may hold values from -72 to 72
- monarch_inner_factor: bfloat16 [3, 64, 64, 64], replicated, may hold values from -0.75 to 0.75
- monarch_outer_factor: bfloat16 [3, 64, 64, 64], replicated, may hold values from -0.75 to 0.75
- adapter_down_weight: bfloat16 [3, 4096, 16], replicated, may hold values from -0.09375 to 0.09375
- adapter_up_weight: bfloat16 [3, 16, 4096], replicated, may hold values from -1.5 to 1.5
- pattern: int32 [768, 3], P('dp'), parts along dimension 0, may hold values from 2 to 47, as said below
Outputs:
- context: bfloat16 [49152, 4096], P(('dp', 'seq')), parts along dimension 0
The draws below stay inside these ranges and needn't reach their ends.
There are 16 independent parts, one for each index of `dp`. The reference program is written for one: setup_inputs(seed, part) draws one part's arguments, and reference() takes and returns one part's arrays. A program takes and returns all parts, laid end to end along the dimension named above; an argument that names none is the same for every part. Nothing has to cross between parts.
Inputs may be any that keep to these rules, and one draw needn't show every extreme that they name: `pattern`: row b names the random key blocks of query block b. The 9 entries of the rows of one index of seq name at most 1 block held by any one index of seq, and exactly 1 of some index's blocks. A block may be named more than once.
All inputs are finite; a program needn't handle non-finite values.
Results may differ from the reference program's by a relative error of at most 0.012.
The reference program's roundings to bfloat16 on the way count: a program that leaves them out, or rounds other values in their place, can miss the bound.
Values may be sent and summed in bfloat16 or wider, within the bound.
No kernel may reach another device: no remote copies, remote signals or barrier semaphores. Data moves between devices by JAX's collectives and lax.ppermute only.
A program may use at most 192 MiB of HBM per device.

```python
import jax
import jax.numpy as jnp
from jax import lax

MODEL_WIDTH = 4096
HEADS = 32
HD = 128
MB = 64
ADAPTER_RANK = 16
BLK = 64
RAND = 3
GLOB_BLOCKS = 2
GLOBAL = 128
QB = 3
DOC = 3072
NB = 48
CAP = 1
N_SEQ = 16


def draw_tokens(key, part):
    values = jax.random.truncated_normal(key, -6.0, 6.0, (DOC, MODEL_WIDTH), jnp.float32)
    return values.astype(jnp.bfloat16)


def draw_pattern(key, part):
    request_count = QB * RAND

    def for_device(device):
        device_key = jax.random.fold_in(key, device)
        orderings = [jax.random.permutation(jax.random.fold_in(device_key, slot), N_SEQ) for slot in range(CAP)]
        sources = jnp.concatenate(orderings)[:request_count].astype(jnp.int32)
        raw_draw = jax.random.randint(jax.random.fold_in(device_key, CAP + 7), (request_count,), 0, 1048576, jnp.int32)
        lowest = jnp.where(sources == 0, GLOB_BLOCKS, 0).astype(jnp.int32)
        within = lowest + raw_draw % (QB - lowest)
        return sources * QB + within
    picked = jax.vmap(for_device)(jnp.arange(N_SEQ, dtype=jnp.int32))
    return picked.reshape(NB, RAND).astype(jnp.int32)


def bell_draw(stream_key, dims, deviation, reach, held_as=jnp.bfloat16):
    drawn = deviation * jax.random.normal(stream_key, dims, jnp.float32)
    return jnp.clip(drawn, min=-reach, max=reach).astype(held_as)


def setup_inputs(seed: int = 0, part: int = 0) -> dict:
    streams_of = jax.random.split(jax.random.key(seed), 7)
    part_splits = jax.random.split(jax.random.fold_in(streams_of[6], part), 7)
    tokens = draw_tokens(jax.random.fold_in(jax.random.fold_in(streams_of[6], part), 71), part)
    monarch_inner_factor = bell_draw(streams_of[1], (3, MB, MB, MB), MB ** -0.5, 0.75)
    monarch_outer_factor = bell_draw(streams_of[2], (3, MB, MB, MB), MB ** -0.5, 0.75)
    adapter_down_weight = bell_draw(streams_of[3], (3, MODEL_WIDTH, ADAPTER_RANK), MODEL_WIDTH ** -0.5, 0.09375)
    adapter_up_weight = bell_draw(streams_of[4], (3, ADAPTER_RANK, MODEL_WIDTH), ADAPTER_RANK ** -0.5, 1.5)
    pattern = draw_pattern(jax.random.fold_in(jax.random.fold_in(streams_of[6], part), 71), part)
    return dict(tokens=tokens, monarch_inner_factor=monarch_inner_factor, monarch_outer_factor=monarch_outer_factor, adapter_down_weight=adapter_down_weight, adapter_up_weight=adapter_up_weight, pattern=pattern)


def finalize_rows(values):
    return lax.optimization_barrier(values.astype(jnp.bfloat16)).astype(jnp.float32)


def apply_projection(tokens, monarch_inner_factor, monarch_outer_factor, adapter_down_weight, adapter_up_weight):
    row_count = tokens.shape[0]
    split_rows = tokens.reshape(row_count, MB, MB).astype(jnp.float32)
    inner_rows = jnp.einsum('tai,paij->ptaj', split_rows, monarch_inner_factor.astype(jnp.float32))
    main_part = jnp.einsum('ptaj,pjak->ptjk', finalize_rows(inner_rows), monarch_outer_factor.astype(jnp.float32))
    adapter_update = jnp.einsum('kg,vgj->vkj', tokens.astype(jnp.float32), adapter_down_weight.astype(jnp.float32))
    adapter_lifted_rows = jnp.einsum('bcj,bjf->bcf', finalize_rows(adapter_update), adapter_up_weight.astype(jnp.float32))
    return (main_part.reshape(3, row_count, MODEL_WIDTH) + adapter_lifted_rows).astype(jnp.bfloat16)


def attend(query_rows, key_rows, value_rows, key_valid):
    scores = jnp.einsum('qhe,khe->hqk', query_rows, key_rows) * (float(HD) ** -0.5)
    scores = jnp.where(key_valid[None, None, :], scores, -jnp.inf)
    row_peak = jnp.max(scores, axis=-1, keepdims=True)
    weights = jnp.exp(scores - row_peak)
    row_total = jnp.sum(weights, axis=-1)
    mixed_sum = jnp.einsum('hqk,khe->qhe', finalize_rows(weights), value_rows)
    result = mixed_sum / jnp.transpose(row_total)[:, :, None]
    return result.reshape(query_rows.shape[0], MODEL_WIDTH).astype(jnp.bfloat16)


def reference(tokens, monarch_inner_factor, monarch_outer_factor, adapter_down_weight, adapter_up_weight, pattern):
    projected_rows = apply_projection(tokens, monarch_inner_factor, monarch_outer_factor, adapter_down_weight, adapter_up_weight)
    query_heads = projected_rows[0].astype(jnp.float32).reshape(DOC, HEADS, HD)
    key_heads = projected_rows[1].astype(jnp.float32).reshape(DOC, HEADS, HD)
    value_heads = projected_rows[2].astype(jnp.float32).reshape(DOC, HEADS, HD)
    offsets = jnp.arange(BLK, dtype=jnp.int32)
    global_ids = jnp.arange(GLOBAL, dtype=jnp.int32)

    def one_block(block_pair):
        block_id = block_pair[0]
        picked = block_pair[1].astype(jnp.int32)
        window_blocks = block_id + jnp.arange(-1, 2, dtype=jnp.int32)
        window_valid = (window_blocks >= GLOB_BLOCKS) & (window_blocks < NB)
        window_ids = (jnp.clip(window_blocks, 0, NB - 1)[:, None] * BLK + offsets[None, :]).reshape(-1)
        random_ids = (picked[:, None] * BLK + offsets[None, :]).reshape(-1)
        key_ids = jnp.concatenate([global_ids, window_ids, random_ids]).astype(jnp.int32)
        key_valid = jnp.concatenate([global_ids >= 0, jnp.repeat(window_valid, BLK), random_ids >= 0])
        query_rows = lax.dynamic_slice_in_dim(query_heads, (block_id * BLK).astype(jnp.int32), BLK, 0)
        return attend(query_rows, key_heads[key_ids], value_heads[key_ids], key_valid)

    block_outs = lax.map(one_block, (jnp.arange(NB, dtype=jnp.int32), pattern))
    context = block_outs.reshape(DOC, MODEL_WIDTH)
    all_valid = jnp.arange(DOC, dtype=jnp.int32) >= 0
    head_rows = attend(query_heads[:GLOBAL], key_heads, value_heads, all_valid)
    return jnp.concatenate([head_rows, context[GLOBAL:]], axis=0)
```

```python
import functools

import jax
import jax.numpy as jnp
from jax import lax
from jax.experimental import pallas as pl
from jax.experimental.pallas import tpu as pltpu
from jax.sharding import PartitionSpec as P

HEADS = 32
HD = 128
BLK = 64
RAND = 3
GLOB_BLOCKS = 2
WIDTH = 4096
MB = 64
RANK = 16
TILE = 256
PAIRS = MB // 2
DEPTH = 2 * MB + RANK
CHIPS = 8
SHARD = 192
DOC = 3072
HGROUP = 4
HWIDTH = HGROUP * HD
HALF = SHARD // 2


def project_body(sizes, first, count, row0, with_query, alias, *refs):
    pieces = len(sizes)
    rows = sum(sizes)
    tiles = (rows + TILE - 1) // TILE
    x_hbm = refs[:pieces]
    w_in, w_out, w_down = refs[pieces : pieces + 3]
    rest = refs[pieces + 3 + (1 if alias else 0) :]
    kv_hbm = rest[0]
    q_hbm = rest[1] if with_query else None
    x_v, mid, out_v, in_sem, out_sem = rest[2 if with_query else 1 :]

    offset = 0
    copies = []
    for piece in range(pieces):
        copy = pltpu.make_async_copy(
            x_hbm[piece], x_v.at[pl.ds(offset, sizes[piece]), :], in_sem.at[piece]
        )
        copy.start()
        copies.append(copy)
        offset += sizes[piece]
    for copy in copies:
        copy.wait()

    def out_copies(tile, height, start):
        result = []
        for p in range(count):
            proj = first + p
            src = out_v.at[tile, p, pl.ds(0, height), :]
            if proj == 0:
                height_q = min(height, SHARD)
                if isinstance(start, int) and start == 0:
                    result.append(
                        pltpu.make_async_copy(
                            out_v.at[tile, p, pl.ds(0, height_q), :], q_hbm, out_sem.at[tile, p]
                        )
                    )
            else:
                dst = kv_hbm.at[proj - 1, pl.ds(row0 + start, height), :]
                result.append(pltpu.make_async_copy(src, dst, out_sem.at[tile, p]))
        return result

    started = []
    for tile in range(tiles):
        x_rows = pl.ds(tile * TILE, TILE)
        low = lax.dot_general(
            w_down[pl.ds(first * RANK, count * RANK), :],
            x_v[x_rows, :],
            (((1,), (1,)), ((), ())),
            preferred_element_type=jnp.float32,
        ).astype(jnp.bfloat16)

        def inner_step(g, carry, x_rows=x_rows):
            cols = pl.ds(pl.multiple_of(g * 128, 128), 128)
            xg = x_v[x_rows, cols]
            for p in range(count):
                part = lax.dot_general(
                    w_in[first + p, g],
                    xg,
                    (((1,), (1,)), ((), ())),
                    preferred_element_type=jnp.float32,
                )
                for half in range(TILE // 128):
                    mid[half, pl.ds(pl.multiple_of(p * WIDTH + g * 128, 128), 128), :] = part[
                        :, half * 128 : (half + 1) * 128
                    ]
            return carry

        lax.fori_loop(0, PAIRS, inner_step, 0, unroll=4)

        def outer_step(h, carry, tile=tile, low=low):
            cols = pl.ds(pl.multiple_of(h * 128, 128), 128)
            for p in range(count):
                for half in range(TILE // 128):
                    one = mid[half, pl.ds(p * WIDTH + 2 * h, MB, stride=MB), :]
                    two = mid[half, pl.ds(p * WIDTH + 2 * h + 1, MB, stride=MB), :]
                    stack = jnp.concatenate(
                        [
                            one.astype(jnp.bfloat16),
                            two.astype(jnp.bfloat16),
                            low[p * RANK : (p + 1) * RANK, half * 128 : (half + 1) * 128],
                        ],
                        axis=0,
                    )
                    done = lax.dot_general(
                        stack,
                        w_out[first + p, h],
                        (((0,), (0,)), ((), ())),
                        preferred_element_type=jnp.float32,
                    )
                    out_v[tile, p, half * 128 : (half + 1) * 128, cols] = done.astype(jnp.bfloat16)
            return carry

        lax.fori_loop(0, HEADS, outer_step, 0, unroll=2)
        height = min(TILE, rows - tile * TILE)
        for copy in out_copies(tile, height, tile * TILE):
            copy.start()
            started.append(copy)
    for copy in started:
        copy.wait()


def project(pieces, weights, row0, with_query=False, kv=None):
    sizes = tuple(piece.shape[0] for piece in pieces)
    rows = sum(sizes)
    tiles = (rows + TILE - 1) // TILE
    first, count = (0, 3) if with_query else (1, 2)
    any_spec = pl.BlockSpec(memory_space=pl.ANY)
    vmem = pl.BlockSpec(memory_space=pltpu.VMEM)
    operands = list(pieces) + list(weights)
    in_specs = [any_spec] * len(pieces) + [vmem] * 3
    aliases = {}
    if kv is not None:
        aliases = {len(operands): 0}
        operands.append(kv)
        in_specs.append(any_spec)
    out_shape = [jax.ShapeDtypeStruct((2, DOC, WIDTH), jnp.bfloat16)]
    if with_query:
        out_shape.append(jax.ShapeDtypeStruct((SHARD, WIDTH), jnp.bfloat16))
    out = pl.pallas_call(
        functools.partial(
            project_body, sizes, first, count, row0, with_query, kv is not None
        ),
        out_shape=tuple(out_shape),
        in_specs=in_specs,
        out_specs=tuple([any_spec] * len(out_shape)),
        input_output_aliases=aliases,
        scratch_shapes=[
            pltpu.VMEM((tiles * TILE, WIDTH), jnp.bfloat16),
            pltpu.VMEM((TILE // 128, count * WIDTH, 128), jnp.float32),
            pltpu.VMEM((tiles, count, TILE, WIDTH), jnp.bfloat16),
            pltpu.SemaphoreType.DMA((len(pieces),)),
            pltpu.SemaphoreType.DMA((tiles, count)),
        ],
        compiler_params=pltpu.CompilerParams(vmem_limit_bytes=60 * 1024 * 1024),
        cost_estimate=pl.CostEstimate(
            flops=rows * count * WIDTH * 64 * 64, bytes_accessed=rows * WIDTH * 6, transcendentals=0
        ),
        name="project",
    )(*operands)
    return out


LOCAL_BLOCKS = 3
KEY_SLOTS = GLOB_BLOCKS + 2 + LOCAL_BLOCKS + LOCAL_BLOCKS * RAND


def softmax_mix(q, keys, values, bias):
    scores = lax.dot_general(
        q, keys, (((1,), (1,)), ((), ())), preferred_element_type=jnp.float32
    ) * (float(HD) ** -0.5)
    if bias is not None:
        scores = scores + bias
    peak = jnp.max(scores, axis=-1, keepdims=True)
    weights = jnp.exp(scores - peak)
    total = jnp.sum(weights, axis=-1, keepdims=True)
    numer = jnp.dot(weights.astype(jnp.bfloat16), values, preferred_element_type=jnp.float32)
    return (numer / total).astype(jnp.bfloat16)


def attend_body(table, flags, q_ref, *refs):
    keys = refs[:KEY_SLOTS]
    values = refs[KEY_SLOTS : 2 * KEY_SLOTS]
    kv_hbm = refs[2 * KEY_SLOTS]
    out_ref = refs[2 * KEY_SLOTS + 1]
    all_kv, sem = refs[2 * KEY_SLOTS + 2 :]
    group = pl.program_id(0)
    is_head = flags[0] == 1

    def fetch(step):
        slot = lax.rem(step, 2)
        cols = pl.ds(pl.multiple_of(step * HWIDTH, HWIDTH), HWIDTH)
        return pltpu.make_async_copy(kv_hbm.at[:, :, cols], all_kv.at[slot], sem.at[slot])

    @pl.when(is_head & (group == 0))
    def _():
        fetch(0).start()

    @pl.when(is_head & (group + 1 < pl.num_programs(0)))
    def _():
        fetch(group + 1).start()

    lane = lax.broadcasted_iota(jnp.int32, (1, 8 * BLK), 1)

    def local(b):
        low_ok, high_ok = flags[1 + 2 * b], flags[2 + 2 * b]
        blocked = ((lane >= 128) & (lane < 192) & (low_ok == 0)) | (
            (lane >= 256) & (lane < 320) & (high_ok == 0)
        )
        bias = jnp.where(blocked, -jnp.inf, 0.0)
        order = [0, 1, 2 + b, 3 + b, 4 + b] + [7 + 3 * b + r for r in range(RAND)]
        for h in range(HGROUP):
            cols = slice(h * HD, (h + 1) * HD)
            k = jnp.concatenate([keys[n][0, :, cols] for n in order], axis=0)
            v = jnp.concatenate([values[n][0, :, cols] for n in order], axis=0)
            q = q_ref[b * BLK : (b + 1) * BLK, cols]
            out_ref[b * BLK : (b + 1) * BLK, cols] = softmax_mix(q, k, v, bias)

    for b in range(LOCAL_BLOCKS):
        if b < GLOB_BLOCKS:
            pl.when(jnp.logical_not(is_head))(functools.partial(local, b))
        else:
            local(b)

    @pl.when(is_head)
    def _():
        slot = lax.rem(group, 2)
        fetch(group).wait()
        for h in range(HGROUP):
            cols = slice(h * HD, (h + 1) * HD)
            q = q_ref[0 : GLOB_BLOCKS * BLK, cols]
            out_ref[0 : GLOB_BLOCKS * BLK, cols] = softmax_mix(
                q, all_kv[slot, 0, :, cols], all_kv[slot, 1, :, cols], None
            )


def attend(table, flags, q, kv):
    def block(plane, n):
        return pl.BlockSpec(
            (1, BLK, HWIDTH), lambda g, table, flags, plane=plane, n=n: (plane, table[n], g)
        )

    row_spec = pl.BlockSpec((SHARD, HWIDTH), lambda g, table, flags: (0, g))
    return pl.pallas_call(
        attend_body,
        out_shape=jax.ShapeDtypeStruct((SHARD, WIDTH), jnp.bfloat16),
        grid_spec=pltpu.PrefetchScalarGridSpec(
            num_scalar_prefetch=2,
            grid=(HEADS // HGROUP,),
            in_specs=[row_spec]
            + [block(0, n) for n in range(KEY_SLOTS)]
            + [block(1, n) for n in range(KEY_SLOTS)]
            + [pl.BlockSpec(memory_space=pl.ANY)],
            out_specs=row_spec,
            scratch_shapes=[
                pltpu.VMEM((2, 2, DOC, HWIDTH), jnp.bfloat16),
                pltpu.SemaphoreType.DMA((2,)),
            ],
        ),
        compiler_params=pltpu.CompilerParams(vmem_limit_bytes=60 * 1024 * 1024),
        name="attend",
    )(table, flags, q, *([kv] * (2 * KEY_SLOTS + 1)))


def prepare_weights(inner, outer, down, up):
    def pair_diagonal(blocks):
        pairs = blocks.reshape(3, PAIRS, 2, MB, MB)
        zero = jnp.zeros_like(pairs[:, :, 0])
        top = jnp.concatenate([pairs[:, :, 0], zero], axis=3)
        bottom = jnp.concatenate([zero, pairs[:, :, 1]], axis=3)
        return jnp.concatenate([top, bottom], axis=2)

    w_in = pair_diagonal(jnp.transpose(inner, (0, 1, 3, 2)))
    lifted = jnp.transpose(up.reshape(3, RANK, HEADS, HD), (0, 2, 1, 3))
    w_out = jnp.concatenate([pair_diagonal(outer), lifted], axis=2)
    w_down = jnp.transpose(down, (0, 2, 1)).reshape(3 * RANK, WIDTH)
    return w_in, w_out, w_down


POSITION = ((0, 1), (3, 5), (7, 9), (11, 13), (14, 15), (10, 12), (6, 8), (2, 4))


def shift(step):
    return [
        (z * 2 + c, ((z + step) % CHIPS) * 2 + c) for z in range(CHIPS) for c in range(2)
    ]


SWAP = [(i, i ^ 1) for i in range(2 * CHIPS)]


def per_device(tokens, inner, outer, down, up, pattern):
    seq = lax.axis_index("seq")
    chip, core = seq // 2, seq % 2
    weights = prepare_weights(inner, outer, down, up)

    def swap(value):
        return lax.ppermute(value, "seq", SWAP)

    partner = swap(tokens)
    steps = []
    forward = backward = tokens
    for step in range(1, CHIPS // 2 + 1):
        if step == CHIPS // 2:
            forward, backward = forward[:HALF], backward[HALF:]
        forward = lax.ppermute(forward, "seq", shift(1))
        backward = lax.ppermute(backward, "seq", shift(-1))
        steps.append((forward, backward))

    kv, q = project((tokens, partner), weights, 0, with_query=True)
    for step, (forward, backward) in enumerate(steps):
        other = (swap(forward), swap(backward))
        (kv,) = project((forward, backward) + other, weights, (2 + 4 * step) * SHARD, kv=kv)

    position = jnp.asarray(POSITION, jnp.int32).reshape(-1)

    def row_block(block):
        source = block // LOCAL_BLOCKS
        distance = (source // 2 - chip) % CHIPS
        other_class = (source % 2) ^ core
        return position[distance * 2 + other_class] * LOCAL_BLOCKS + block % LOCAL_BLOCKS

    first_block = seq * LOCAL_BLOCKS
    block_total = 2 * CHIPS * LOCAL_BLOCKS
    mine = lax.dynamic_slice_in_dim(pattern, first_block, LOCAL_BLOCKS, 0).reshape(-1)
    window = (first_block - 1 + jnp.arange(LOCAL_BLOCKS + 2)) % block_total
    table = row_block(
        jnp.concatenate([jnp.arange(GLOB_BLOCKS), window, mine]).astype(jnp.int32)
    ).astype(jnp.int32)
    ids = first_block + jnp.arange(LOCAL_BLOCKS)
    low_ok = ids - 1 >= GLOB_BLOCKS
    high_ok = ids + 1 < block_total
    flags = jnp.concatenate(
        [(seq == 0)[None], jnp.stack([low_ok, high_ok], axis=1).reshape(-1)]
    ).astype(jnp.int32)
    return attend(table, flags, q, kv)


def solution(mesh):
    return jax.shard_map(
        per_device,
        mesh=mesh,
        in_specs=(P(("dp", "seq"), None), P(), P(), P(), P(), P("dp", None)),
        out_specs=P(("dp", "seq"), None),
        check_vma=False,
    )
```

```python
import functools

import jax
import jax.numpy as jnp
from jax import lax
from jax.experimental import pallas as pl
from jax.experimental.pallas import tpu as pltpu
from jax.sharding import PartitionSpec as P

HEADS = 32
HD = 128
BLK = 64
RAND = 3
GLOB_BLOCKS = 2
WIDTH = 4096
MB = 64
RANK = 16
TILE = 256
GTILE = 384
UNROLL_OUT = 4
PAIRS = MB // 2
CHIPS = 8
LOCAL_BLOCKS = 3
SHARD = LOCAL_BLOCKS * BLK
DOC = 3072
PITCH = 72
GLOBAL_ROWS = GLOB_BLOCKS * BLK
OWN_COLS = WIDTH // (2 * CHIPS)
KV_ROWS = 1536


def project_tile(first, count, low_of, x_of, w_in, w_out, mid, out_v):
    low = low_of()

    def inner_step(g, carry):
        xg = x_of(pl.ds(pl.multiple_of(g * 128, 128), 128))
        for p in range(count):
            part = lax.dot_general(
                w_in[first + p, g],
                xg,
                (((1,), (1,)), ((), ())),
                preferred_element_type=jnp.float32,
            )
            for a in range(2):
                start = pl.multiple_of((p * MB + 2 * g + a) * PITCH, 8)
                for lanes in range(TILE // 128):
                    mid[lanes, pl.ds(start, MB), :] = part[
                        a * MB : (a + 1) * MB, lanes * 128 : (lanes + 1) * 128
                    ]
        return carry

    lax.fori_loop(0, PAIRS, inner_step, 0, unroll=8)

    def outer_step(h, carry):
        cols = pl.ds(pl.multiple_of(h * 128, 128), 128)
        for p in range(count):
            base = p * MB * PITCH + 2 * h
            parts = []
            for lanes in range(TILE // 128):
                one = mid[lanes, pl.ds(base, MB, stride=PITCH), :]
                two = mid[lanes, pl.ds(base + 1, MB, stride=PITCH), :]
                parts.append(
                    jnp.concatenate([one.astype(jnp.bfloat16), two.astype(jnp.bfloat16)], axis=0)
                )
            stack = jnp.concatenate(
                [jnp.concatenate(parts, axis=1), low[p * RANK : (p + 1) * RANK]], axis=0
            )
            done = lax.dot_general(
                stack,
                w_out[first + p, h],
                (((0,), (0,)), ((), ())),
                preferred_element_type=jnp.float32,
            )
            out_v[p, :, cols] = done.astype(jnp.bfloat16)
        return carry

    lax.fori_loop(0, HEADS, outer_step, 0, unroll=UNROLL_OUT)


def named_block(info, source):
    block = jnp.int32(0)
    for r in range(LOCAL_BLOCKS * RAND):
        named = info[1 + r]
        block = jnp.where(lax.div(named, LOCAL_BLOCKS) == source, lax.rem(named, LOCAL_BLOCKS), block)
    return block


def source_of(info, offset):
    dz, cls = offset
    chip = lax.rem(lax.div(info[0], 2) + (dz + CHIPS), CHIPS)
    return chip * 2 + lax.rem(info[0] + cls, 2)


def step_rows(info, kind, pieces):
    core = lax.rem(info[0], 2)
    if kind == 0:
        near = SHARD + jnp.where(core == 0, 0, 2 * BLK)
        glob = jnp.where(info[0] == 0, 0, jnp.where(info[0] == 1, SHARD, -1))
        return [0, BLK, 2 * BLK, near], glob
    if kind == CHIPS // 2:
        offsets = [(kind, 0), (kind, 1)]
    else:
        offsets = [(-kind, 0), (kind, 0), (-kind, 1), (kind, 1)]
    starts = []
    glob = jnp.int32(-1)
    for n, offset in enumerate(offsets):
        source = source_of(info, offset)
        starts.append(n * SHARD + BLK * named_block(info, source))
        glob = jnp.where(source == 0, n * SHARD, glob)
    if kind == 2:
        partner = info[0] + 1 - 2 * core
        starts += [4 * SHARD + BLK * named_block(info, partner), 6 * SHARD, 0, 0]
    if kind == CHIPS // 2:
        there = jnp.where(glob >= 0, glob, pieces * SHARD)
        starts += [there, there + BLK]
    return starts, glob


def own_project(x, own_in, own_out, w_down, first, count):
    wide = count * OWN_COLS
    inner = jnp.dot(x, own_in[...], preferred_element_type=jnp.float32)
    low = lax.dot_general(
        x,
        w_down[first * RANK : (first + count) * RANK, :],
        (((1,), (1,)), ((), ())),
        preferred_element_type=jnp.float32,
    )
    main = jnp.dot(inner.astype(jnp.bfloat16), own_out[0:wide, :], preferred_element_type=jnp.float32)
    lifted = jnp.dot(
        low.astype(jnp.bfloat16),
        own_out[wide : wide + count * RANK, :],
        preferred_element_type=jnp.float32,
    )
    return (main + lifted).astype(jnp.bfloat16)


def step_body(kind, pieces, tiles, carried, with_own, row0, own0, alias, info, *refs):
    x_hbm = refs[: len(pieces)]
    at = len(pieces)
    w_in, w_out, w_down = refs[at : at + 3]
    at += 3
    if with_own:
        own_in, own_out = refs[at : at + 2]
        at += 2
    gx_in = refs[at + len(alias) - 1] if alias else None
    at += len(alias)
    kv_hbm = refs[at]
    at += 1
    if with_own:
        own_hbm = refs[at]
        at += 1
    else:
        q_hbm = refs[at]
        at += 1
    gx_hbm = refs[at]
    x_v, slots_v, mid, out_v, own_v, in_sem, out_sem, own_sem, gx_sem = refs[at + 1 :]
    rows = sum(pieces) // GTILE * GTILE
    first, count = (1, 2) if with_own else (0, 3)
    starts, glob = step_rows(info, kind, len(pieces))

    copies = [
        pltpu.make_async_copy(
            x_hbm[n], x_v.at[pl.ds(n * SHARD, pieces[n]), :], in_sem.at[n]
        )
        for n in range(len(pieces))
    ]
    for copy in copies:
        copy.start()
    if carried:
        carry_copy = pltpu.make_async_copy(
            gx_in, x_v.at[pl.ds(rows, GLOBAL_ROWS), :], in_sem.at[len(pieces)]
        )
        carry_copy.start()
        carry_copy.wait()
    for copy in copies:
        copy.wait()

    gx_copy = pltpu.make_async_copy(
        x_v.at[pl.ds(pl.multiple_of(jnp.maximum(glob, 0), BLK), GLOBAL_ROWS), :], gx_hbm, gx_sem
    )

    @pl.when(glob >= 0)
    def _():
        gx_copy.start()

    out_copies = []
    for tile in range(tiles):
        for n in range(TILE // BLK):
            start = pl.multiple_of(starts[4 * tile + n], BLK)

            def move(c, carry, n=n, start=start):
                cols = pl.ds(pl.multiple_of(c * 512, 512), 512)
                slots_v[n * BLK : (n + 1) * BLK, cols] = x_v[pl.ds(start, BLK), cols]
                return carry

            lax.fori_loop(0, WIDTH // 512, move, 0)

        def low_of():
            return lax.dot_general(
                w_down[pl.ds(first * RANK, count * RANK), :],
                slots_v[...],
                (((1,), (1,)), ((), ())),
                preferred_element_type=jnp.float32,
            ).astype(jnp.bfloat16)

        project_tile(
            first, count, low_of, lambda cols: slots_v[:, cols], w_in, w_out, mid, out_v.at[tile]
        )
        for p in range(count):
            if first + p == 0:
                src, dst = out_v.at[tile, p, pl.ds(0, SHARD), :], q_hbm
            else:
                src = out_v.at[tile, p]
                dst = kv_hbm.at[first + p - 1, pl.ds(row0 + tile * TILE, TILE), :]
            copy = pltpu.make_async_copy(src, dst, out_sem.at[tile, p])
            copy.start()
            out_copies.append(copy)

    if with_own:

        def own_step(i, carry):
            span = pl.ds(pl.multiple_of(i * GTILE, GTILE), GTILE)
            own_v[span, :] = own_project(x_v[span, :], own_in, own_out, w_down, 1, 2)
            return carry

        lax.fori_loop(0, rows // GTILE, own_step, 0)
        own_copy = pltpu.make_async_copy(own_v, own_hbm.at[pl.ds(own0, rows), :], own_sem)
        own_copy.start()
        own_copy.wait()
    for copy in out_copies:
        copy.wait()

    @pl.when(glob >= 0)
    def _():
        gx_copy.wait()


def gather_step(kind, info, pieces, weights, own_weights, row0, own0, tiles, carried, previous):
    count = len(pieces)
    sizes = tuple(piece.shape[0] for piece in pieces)
    rows = sum(sizes) // GTILE * GTILE
    with_own = own_weights is not None
    any_spec = pl.BlockSpec(memory_space=pl.ANY)
    vmem = pl.BlockSpec(memory_space=pltpu.VMEM)
    operands = list(pieces) + list(weights) + (list(own_weights) if with_own else [])
    in_specs = [any_spec] * count + [vmem] * (len(operands) - count)
    kv_shape = jax.ShapeDtypeStruct((2, KV_ROWS, WIDTH), jnp.bfloat16)
    gx_shape = jax.ShapeDtypeStruct((GLOBAL_ROWS, WIDTH), jnp.bfloat16)
    if with_own:
        second = jax.ShapeDtypeStruct((DOC, 2 * OWN_COLS), jnp.bfloat16)
    else:
        second = jax.ShapeDtypeStruct((SHARD, WIDTH), jnp.bfloat16)
    alias = tuple((value, out) for value, out in previous)
    aliases = {}
    for value, out in alias:
        aliases[1 + len(operands)] = out
        operands.append(value)
        in_specs.append(any_spec)
    projections = 2 if with_own else 3
    return pl.pallas_call(
        functools.partial(
            step_body, kind, sizes, tiles, carried, with_own, row0, own0, tuple(o for _, o in alias)
        ),
        out_shape=(kv_shape, second, gx_shape),
        grid_spec=pltpu.PrefetchScalarGridSpec(
            num_scalar_prefetch=1,
            grid=(),
            in_specs=in_specs,
            out_specs=(any_spec,) * 3,
            scratch_shapes=[
                pltpu.VMEM((sum(sizes) + (GLOBAL_ROWS if carried else 0), WIDTH), jnp.bfloat16),
                pltpu.VMEM((TILE, WIDTH), jnp.bfloat16),
                pltpu.VMEM((TILE // 128, projections * MB * PITCH, 128), jnp.float32),
                pltpu.VMEM((tiles, projections, TILE, WIDTH), jnp.bfloat16),
                pltpu.VMEM((rows, 2 * OWN_COLS), jnp.bfloat16),
                pltpu.SemaphoreType.DMA((count + 1,)),
                pltpu.SemaphoreType.DMA((tiles, projections)),
                pltpu.SemaphoreType.DMA(()),
                pltpu.SemaphoreType.DMA(()),
            ],
        ),
        input_output_aliases=aliases,
        compiler_params=pltpu.CompilerParams(vmem_limit_bytes=46 * 1024 * 1024),
        cost_estimate=pl.CostEstimate(
            flops=tiles * 8 * 10**9, bytes_accessed=20 * 10**6, transcendentals=0
        ),
        name="gather_step",
    )(info, *operands)


KEY_SLOTS = GLOB_BLOCKS + 2 + LOCAL_BLOCKS + LOCAL_BLOCKS * RAND
WINDOW_ROW = GLOB_BLOCKS * BLK
RANDOM_ROW = WINDOW_ROW + (LOCAL_BLOCKS + 2) * BLK
LOCAL_COLS = 1024
EXP_SCALE = float(HD) ** -0.5 * 1.4426950408889634


def softmax_mix(q, keys, values, bias):
    scores = lax.dot_general(q, keys, (((1,), (1,)), ((), ())), preferred_element_type=jnp.float32)
    if bias is not None:
        scores = scores + bias
    peak = jnp.max(scores, axis=-1, keepdims=True) * EXP_SCALE
    weights = jnp.exp2(scores * EXP_SCALE - peak)
    total = jnp.sum(weights, axis=-1, keepdims=True)
    numer = jnp.dot(weights.astype(jnp.bfloat16), values, preferred_element_type=jnp.float32)
    return (numer * (1.0 / total)).astype(jnp.bfloat16)


def key_blocks(info):
    core = lax.rem(info[0], 2)
    below = jnp.where(core == 0, EDGE_FAR, EDGE_NEAR)
    above = jnp.where(core == 0, EDGE_NEAR, EDGE_FAR)
    blocks = [GLOBAL_SLOT, GLOBAL_SLOT + 1, below, 0, 1, 2, above]
    for r in range(LOCAL_BLOCKS * RAND):
        source = lax.div(info[1 + r], LOCAL_BLOCKS)
        distance = lax.rem(lax.div(source, 2) - lax.div(info[0], 2) + CHIPS, CHIPS)
        other = lax.rem(source + core, 2)
        place = lax.rem(info[1 + r], LOCAL_BLOCKS)
        for d in range(CHIPS):
            for c in range(2):
                if (d, c) != (0, 0):
                    place = jnp.where((distance == d) & (other == c), SLOT[d][c], place)
        blocks.append(place)
    return blocks


def local_body(group, info, q_ref, kv_hbm, out_ref, held, sem):
    blocks = key_blocks(info)
    half = LOCAL_COLS // 2
    copies = []
    for side in range(2):
        for n in range(KEY_SLOTS):
            rows = pl.ds(pl.multiple_of(blocks[n] * BLK, BLK), BLK)
            for plane in range(2):
                copies.append(
                    pltpu.make_async_copy(
                        kv_hbm.at[plane, rows, pl.ds(group * LOCAL_COLS + side * half, half)],
                        held.at[side, plane, pl.ds(n * BLK, BLK), :],
                        sem.at[side, plane, n],
                    )
                )
    for copy in copies:
        copy.start()
    lane = lax.broadcasted_iota(jnp.int32, (1, 8 * BLK), 1)
    biases = []
    for b in range(LOCAL_BLOCKS):
        block = info[0] * LOCAL_BLOCKS + b
        blocked = ((lane >= 128) & (lane < 192) & (block - 1 < GLOB_BLOCKS)) | (
            (lane >= 256) & (lane < 320) & (block + 1 >= DOC // BLK)
        )
        biases.append(jnp.where(blocked, -jnp.inf, 0.0))
    for side in range(2):
        for copy in copies[side * 2 * KEY_SLOTS : (side + 1) * 2 * KEY_SLOTS]:
            copy.wait()
        for h in range(half // HD):
            cols = slice(h * HD, (h + 1) * HD)
            wide = slice(side * half + h * HD, side * half + (h + 1) * HD)
            for b in range(LOCAL_BLOCKS):
                first = WINDOW_ROW + b * BLK
                second = RANDOM_ROW + b * RAND * BLK
                k, v = (
                    jnp.concatenate(
                        [
                            held[side, plane, 0:WINDOW_ROW, cols],
                            held[side, plane, first : first + 3 * BLK, cols],
                            held[side, plane, second : second + RAND * BLK, cols],
                        ],
                        axis=0,
                    )
                    for plane in range(2)
                )
                q = q_ref[b * BLK : (b + 1) * BLK, wide]
                out_ref[b * BLK : (b + 1) * BLK, wide] = softmax_mix(q, k, v, biases[b])


def attend_local(group, info, q, kv):
    return pl.pallas_call(
        functools.partial(local_body, group),
        out_shape=jax.ShapeDtypeStruct((SHARD, LOCAL_COLS), jnp.bfloat16),
        grid_spec=pltpu.PrefetchScalarGridSpec(
            num_scalar_prefetch=1,
            grid=(1,),
            in_specs=[
                pl.BlockSpec((SHARD, LOCAL_COLS), lambda g, info: (0, group)),
                pl.BlockSpec(memory_space=pl.ANY),
            ],
            out_specs=pl.BlockSpec((SHARD, LOCAL_COLS), lambda g, info: (0, 0)),
            scratch_shapes=[
                pltpu.VMEM((2, 2, KEY_SLOTS * BLK, LOCAL_COLS // 2), jnp.bfloat16),
                pltpu.SemaphoreType.DMA((2, 2, KEY_SLOTS)),
            ],
        ),
        compiler_params=pltpu.CompilerParams(vmem_limit_bytes=40 * 1024 * 1024),
        cost_estimate=pl.CostEstimate(
            flops=4 * 10**9, bytes_accessed=5 * 10**6, transcendentals=800000
        ),
        name="attend_local",
    )(info, q, kv)


def global_body(gx, own_in, own_out, w_down, kv_ref, out_ref):
    q = own_project(gx[...], own_in, own_out, w_down, 0, 1)
    for h in range(OWN_COLS // HD):
        cols = slice(h * HD, (h + 1) * HD)
        wide = slice(OWN_COLS + h * HD, OWN_COLS + (h + 1) * HD)
        out_ref[:, cols] = softmax_mix(q[:, cols], kv_ref[:, cols], kv_ref[:, wide], None)


def attend_global(gx, own_query_weights, w_down, own_kv):
    return pl.pallas_call(
        global_body,
        out_shape=jax.ShapeDtypeStruct((GLOBAL_ROWS, OWN_COLS), jnp.bfloat16),
        in_specs=[pl.BlockSpec(memory_space=pltpu.VMEM)] * 5,
        out_specs=pl.BlockSpec(memory_space=pltpu.VMEM),
        compiler_params=pltpu.CompilerParams(vmem_limit_bytes=40 * 1024 * 1024),
        cost_estimate=pl.CostEstimate(
            flops=2 * 10**9, bytes_accessed=8 * 10**6, transcendentals=800000
        ),
        name="attend_global",
    )(gx, *own_query_weights, w_down, own_kv)


def merge_body(info, head, *refs):
    out_ref = refs[-1]
    for group, part in enumerate(refs[:-1]):
        out_ref[:, group * LOCAL_COLS : (group + 1) * LOCAL_COLS] = part[...]

    @pl.when(info[0] == 0)
    def _():
        out_ref[0:GLOBAL_ROWS, :] = head[...]


def merge(info, head, parts):
    return pl.pallas_call(
        merge_body,
        out_shape=jax.ShapeDtypeStruct((SHARD, WIDTH), jnp.bfloat16),
        in_specs=[pl.BlockSpec(memory_space=pltpu.SMEM)]
        + [pl.BlockSpec(memory_space=pltpu.VMEM)] * (1 + len(parts)),
        out_specs=pl.BlockSpec(memory_space=pltpu.VMEM),
        compiler_params=pltpu.CompilerParams(vmem_limit_bytes=40 * 1024 * 1024),
        name="merge",
    )(info, head, *parts)


def main_body(inner, outer, up, w_in, w_out):
    row = lax.broadcasted_iota(jnp.int32, (MB, MB), 0)
    col = lax.broadcasted_iota(jnp.int32, (MB, MB), 1)
    unit = jnp.where(row == col, 1.0, 0.0).astype(jnp.bfloat16)
    lane = lax.broadcasted_iota(jnp.int32, (MB, 2 * MB), 1)
    zero = jnp.zeros((MB, MB), jnp.bfloat16)

    def pair(n, carry):
        p, g = n // PAIRS, n % PAIRS
        blocks = jnp.concatenate([inner[p, 2 * g], inner[p, 2 * g + 1]], axis=0)
        turned = lax.dot_general(
            unit, blocks, (((1,), (1,)), ((), ())), preferred_element_type=jnp.float32
        )
        w_in[p, g, 0:MB, :] = jnp.where(lane < MB, turned, 0.0).astype(jnp.bfloat16)
        w_in[p, g, MB : 2 * MB, :] = jnp.where(lane < MB, 0.0, turned).astype(jnp.bfloat16)
        w_out[p, g, 0:MB, :] = jnp.concatenate([outer[p, 2 * g], zero], axis=1)
        w_out[p, g, MB : 2 * MB, :] = jnp.concatenate([zero, outer[p, 2 * g + 1]], axis=1)
        cols = pl.ds(pl.multiple_of(g * HD, HD), HD)
        w_out[p, g, 2 * MB : 2 * MB + RANK, :] = up[p, :, cols]
        return carry

    lax.fori_loop(0, 3 * PAIRS, pair, 0, unroll=8)


def prepare_weights(inner, outer, down, up):
    vmem = pl.BlockSpec(memory_space=pltpu.VMEM)
    w_in, w_out = pl.pallas_call(
        main_body,
        out_shape=(
            jax.ShapeDtypeStruct((3, PAIRS, 2 * MB, 2 * MB), jnp.bfloat16),
            jax.ShapeDtypeStruct((3, PAIRS, 2 * MB + RANK, HD), jnp.bfloat16),
        ),
        in_specs=[vmem] * 3,
        out_specs=(vmem, vmem),
        compiler_params=pltpu.CompilerParams(vmem_limit_bytes=40 * 1024 * 1024),
        cost_estimate=pl.CostEstimate(flops=10**9, bytes_accessed=12 * 10**6, transcendentals=0),
        name="main_weights",
    )(inner, outer, up)
    return w_in, w_out, jnp.transpose(down, (0, 2, 1)).reshape(3 * RANK, WIDTH)


def own_body(info, inner, outer, up, q_in, q_out, kv_in, kv_out):
    own_j = OWN_COLS // MB
    q_out[...] = jnp.zeros_like(q_out)
    kv_out[...] = jnp.zeros_like(kv_out)
    col = lax.broadcasted_iota(jnp.int32, (MB, OWN_COLS), 1)
    row = lax.broadcasted_iota(jnp.int32, (MB, OWN_COLS), 0)
    pick = jnp.where(row == info[0] * own_j + col // MB, 1.0, 0.0).astype(jnp.bfloat16)
    own_cols = pl.ds(pl.multiple_of(info[0] * OWN_COLS, OWN_COLS), OWN_COLS)
    span = 512
    wide_col = lax.broadcasted_iota(jnp.int32, (span, OWN_COLS), 1) % MB
    wide_row = lax.broadcasted_iota(jnp.int32, (span, OWN_COLS), 0) // MB
    for p, left, right, n, count in ((0, q_in, q_out, 0, 1), (1, kv_in, kv_out, 0, 2), (2, kv_in, kv_out, 1, 2)):

        def fill(i, carry, p=p, left=left, n=n):
            rows = pl.ds(pl.multiple_of(i * span, span), span)
            picked = jnp.dot(inner[p, rows, :], pick, preferred_element_type=jnp.float32)
            here = jnp.where(wide_col == wide_row + i * (span // MB), picked, 0.0)
            left[rows, n * OWN_COLS : (n + 1) * OWN_COLS] = here.astype(jnp.bfloat16)
            return carry

        lax.fori_loop(0, WIDTH // span, fill, 0)
        for j in range(own_j):
            block = outer[p, info[0] * own_j + j]
            at = n * OWN_COLS + j * MB
            right[at : at + MB, at : at + MB] = block
        at = count * OWN_COLS + n * RANK
        right[at : at + RANK, n * OWN_COLS : (n + 1) * OWN_COLS] = up[p, :, own_cols]


def own_head_weights(info, inner, outer, up):
    vmem = pl.BlockSpec(memory_space=pltpu.VMEM)
    two = 2 * OWN_COLS
    shapes = (
        (WIDTH, OWN_COLS),
        (OWN_COLS + RANK, OWN_COLS),
        (WIDTH, two),
        (two + 2 * RANK, two),
    )
    q_in, q_out, kv_in, kv_out = pl.pallas_call(
        own_body,
        out_shape=tuple(jax.ShapeDtypeStruct(shape, jnp.bfloat16) for shape in shapes),
        in_specs=[pl.BlockSpec(memory_space=pltpu.SMEM)] + [vmem] * 3,
        out_specs=(vmem,) * 4,
        compiler_params=pltpu.CompilerParams(vmem_limit_bytes=40 * 1024 * 1024),
        name="own_weights",
    )(info, inner.reshape(3, WIDTH, MB), outer, up)
    return (q_in, q_out), (kv_in, kv_out)


SLOT = ((0, 12), (5, 7), (9, 11), (17, 19), (20, 21), (16, 18), (8, 10), (4, 6))
EDGE_NEAR, EDGE_FAR, GLOBAL_SLOT = 3, 13, 22


def shift(step):
    return [
        (z * 2 + c, ((z + step) % CHIPS) * 2 + c) for z in range(CHIPS) for c in range(2)
    ]


SWAP = [(i, i ^ 1) for i in range(2 * CHIPS)]
SPLIT = [
    (z * 2 + c, ((z + (1 if c == 0 else -1)) % CHIPS) * 2 + c)
    for z in range(CHIPS)
    for c in range(2)
]


def per_device(tokens, inner, outer, down, up, pattern):
    seq = lax.axis_index("seq").astype(jnp.int32)
    core = seq % 2
    mine = lax.dynamic_slice_in_dim(pattern, seq * LOCAL_BLOCKS, LOCAL_BLOCKS, 0).reshape(-1)
    info = jnp.concatenate([seq[None], mine]).astype(jnp.int32)

    def swap(value):
        return lax.ppermute(value, "seq", SWAP)

    def hop(forward, backward):
        return (
            lax.ppermute(forward, "seq", shift(1)),
            lax.ppermute(backward, "seq", shift(-1)),
        )

    partner = swap(tokens)
    forward, backward = hop(tokens, tokens)
    weights = prepare_weights(inner, outer, down, up)
    kv, q, gx = gather_step(0, info, (tokens, partner), weights, None, 0, 0, 1, False, ())
    own_kv = None
    own0 = 0
    for step in range(1, CHIPS // 2):
        if own_kv is None:
            forward, backward, kv, gx, late = lax.optimization_barrier(
                (forward, backward, kv, gx, info)
            )
            own_query, own_kv_weights = own_head_weights(late, inner, outer, up)
        else:
            forward, backward, kv, gx, own_kv = lax.optimization_barrier(
                (forward, backward, kv, gx, own_kv)
            )
        pieces = (forward, backward, swap(forward), swap(backward))
        tiles = 1
        if step == 1:
            edge = jnp.where(core == 0, pieces[2][2 * BLK :], pieces[3][:BLK])
        if step == 2:
            tiles = 2
            pieces += (partner, tokens, edge)
        if step < CHIPS // 2 - 1:
            forward, backward = hop(forward, backward)
        else:
            far = lax.ppermute(jnp.where(core == 0, forward, backward), "seq", SPLIT)
        previous = [(kv, 0)] + ([(own_kv, 1)] if own_kv is not None else []) + [(gx, 2)]
        row0 = {1: 4, 2: 8, 3: 16}[step] * BLK
        kv, own_kv, gx = gather_step(
            step, info, pieces, weights, own_kv_weights, row0, own0, tiles, False, previous
        )
        own0 += len(pieces[:6]) * SHARD
    far, kv, own_kv, gx = lax.optimization_barrier((far, kv, own_kv, gx))
    kv, own_kv, gx = gather_step(
        CHIPS // 2,
        info,
        (far, swap(far)),
        weights,
        own_kv_weights,
        20 * BLK,
        own0,
        1,
        True,
        [(kv, 0), (own_kv, 1), (gx, 2)],
    )

    head = attend_global(gx, own_query, weights[2], own_kv)
    reach = 1
    while reach < 2 * CHIPS:
        pairs = [(i + reach, i) for i in range(0, 2 * CHIPS, 2 * reach)]
        head = jnp.concatenate([head, lax.ppermute(head, "seq", pairs)], axis=1)
        reach *= 2
    parts = [attend_local(g, info, q, kv) for g in range(WIDTH // LOCAL_COLS)]
    return merge(info, head, parts)


def solution(mesh):
    return jax.shard_map(
        per_device,
        mesh=mesh,
        in_specs=(P(("dp", "seq"), None), P(), P(), P(), P(), P("dp", None)),
        out_specs=P(("dp", "seq"), None),
        check_vma=False,
    )
```

```python
import functools

import jax
import jax.numpy as jnp
from jax import lax
from jax.experimental import pallas as pl
from jax.experimental.pallas import tpu as pltpu
from jax.sharding import PartitionSpec as P

HEADS = 32
HD = 128
BLK = 64
RAND = 3
GLOB_BLOCKS = 2
WIDTH = 4096
MB = 64
RANK = 16
TILE = 256
GTILE = 384
GROUP_IN = 8
GROUP_OUT = 4
PAIRS = MB // 2
CHIPS = 8
LOCAL_BLOCKS = 3
SHARD = LOCAL_BLOCKS * BLK
DOC = 3072
PITCH = 72
GLOBAL_ROWS = GLOB_BLOCKS * BLK
OWN_COLS = WIDTH // (2 * CHIPS)
KV_ROWS = 1536


def project_tile(first, count, low_of, x_of, w_in, w_out, mid, out_v):
    low = low_of()

    def inner_step(i, carry):
        made = []
        for n in range(GROUP_IN):
            g = i * GROUP_IN + n
            xg = x_of(pl.ds(pl.multiple_of(g * 128, 128), 128))
            for p in range(count):
                part = lax.dot_general(
                    w_in[first + p, g],
                    xg,
                    (((1,), (1,)), ((), ())),
                    preferred_element_type=jnp.float32,
                )
                made.append((g, p, part))
        for g, p, part in made:
            for a in range(2):
                start = pl.multiple_of((p * MB + 2 * g + a) * PITCH, 8)
                for lanes in range(TILE // 128):
                    mid[lanes, pl.ds(start, MB), :] = part[
                        a * MB : (a + 1) * MB, lanes * 128 : (lanes + 1) * 128
                    ]
        return carry

    lax.fori_loop(0, PAIRS // GROUP_IN, inner_step, 0)

    def outer_step(i, carry):
        units = [(i * GROUP_OUT + n, p) for n in range(GROUP_OUT) for p in range(count)]
        stacks = []
        for h, p in units:
            base = p * MB * PITCH + 2 * h
            parts = []
            for lanes in range(TILE // 128):
                one = mid[lanes, pl.ds(base, MB, stride=PITCH), :]
                two = mid[lanes, pl.ds(base + 1, MB, stride=PITCH), :]
                parts.append(
                    jnp.concatenate([one.astype(jnp.bfloat16), two.astype(jnp.bfloat16)], axis=0)
                )
            stacks.append(
                jnp.concatenate(
                    [jnp.concatenate(parts, axis=1), low[p * RANK : (p + 1) * RANK]], axis=0
                )
            )
        made = [
            lax.dot_general(
                stack,
                w_out[first + p, h],
                (((0,), (0,)), ((), ())),
                preferred_element_type=jnp.float32,
            )
            for stack, (h, p) in zip(stacks, units)
        ]
        for done, (h, p) in zip(made, units):
            out_v[p, :, pl.ds(pl.multiple_of(h * 128, 128), 128)] = done.astype(jnp.bfloat16)
        return carry

    lax.fori_loop(0, HEADS // GROUP_OUT, outer_step, 0)


def named_block(info, source):
    block = jnp.int32(0)
    for r in range(LOCAL_BLOCKS * RAND):
        named = info[1 + r]
        block = jnp.where(lax.div(named, LOCAL_BLOCKS) == source, lax.rem(named, LOCAL_BLOCKS), block)
    return block


def source_of(info, offset):
    dz, cls = offset
    chip = lax.rem(lax.div(info[0], 2) + (dz + CHIPS), CHIPS)
    return chip * 2 + lax.rem(info[0] + cls, 2)


def step_rows(info, kind, pieces):
    core = lax.rem(info[0], 2)
    if kind == 0:
        near = SHARD + jnp.where(core == 0, 0, 2 * BLK)
        glob = jnp.where(info[0] == 0, 0, jnp.where(info[0] == 1, SHARD, -1))
        return [0, BLK, 2 * BLK, near], glob
    if kind == CHIPS // 2:
        offsets = [(kind, 0), (kind, 1)]
    else:
        offsets = [(-kind, 0), (kind, 0), (-kind, 1), (kind, 1)]
    starts = []
    glob = jnp.int32(-1)
    for n, offset in enumerate(offsets):
        source = source_of(info, offset)
        starts.append(n * SHARD + BLK * named_block(info, source))
        glob = jnp.where(source == 0, n * SHARD, glob)
    if kind == 2:
        partner = info[0] + 1 - 2 * core
        starts += [4 * SHARD + BLK * named_block(info, partner), 6 * SHARD, 0, 0]
    if kind == CHIPS // 2:
        starts += [pieces * SHARD, pieces * SHARD + BLK]
    return starts, glob


def own_query(x, own_in, own_out, w_down):
    inner = jnp.dot(x, own_in[...], preferred_element_type=jnp.float32)
    low = lax.dot_general(
        x, w_down[0:RANK, :], (((1,), (1,)), ((), ())), preferred_element_type=jnp.float32
    )
    main = jnp.dot(
        inner.astype(jnp.bfloat16), own_out[0:OWN_COLS, :], preferred_element_type=jnp.float32
    )
    lifted = jnp.dot(
        low.astype(jnp.bfloat16), own_out[OWN_COLS:, :], preferred_element_type=jnp.float32
    )
    return (main + lifted).astype(jnp.bfloat16)


def own_keys_values(x_v, span, own_in, own_out):
    quarter = WIDTH // 4
    parts, low = [], None
    for n in range(4):
        cols = slice(n * quarter, (n + 1) * quarter)
        part = jnp.dot(x_v[span, cols], own_in[cols, :], preferred_element_type=jnp.float32)
        parts.append(part[:, 0:128].astype(jnp.bfloat16))
        low = part[:, 128:256] if low is None else low + part[:, 128:256]
    parts.append(low.astype(jnp.bfloat16))
    inner = jnp.concatenate(parts, axis=1)
    return jnp.dot(inner, own_out[...], preferred_element_type=jnp.float32).astype(jnp.bfloat16)


def step_body(kind, pieces, tiles, mode, row0, own0, alias, info, *refs):
    x_hbm = refs[: len(pieces)]
    at = len(pieces)
    with_own, carried = mode == "both", mode == "slots"
    w_in, w_out, w_down = refs[at : at + 3]
    at += 3
    if with_own:
        own_in, own_out = refs[at : at + 2]
        at += 2
    gx_in = refs[at + alias - 1] if alias else None
    at += alias
    kv_hbm = refs[at]
    at += 1
    if with_own:
        own_hbm = refs[at]
        at += 1
    if mode == "query":
        q_hbm = refs[at]
        at += 1
    if not carried:
        gx_hbm = refs[at]
        at += 1
    x_v, slots_v, mid, out_v, own_v, in_sem, out_sem, own_sem, gx_sem = refs[at:]
    rows = sum(pieces) // GTILE * GTILE
    first, count = (0, 3) if mode == "query" else (1, 2)
    starts, glob = step_rows(info, kind, len(pieces))

    copies = [
        pltpu.make_async_copy(
            x_hbm[n], x_v.at[pl.ds(n * SHARD, pieces[n]), :], in_sem.at[n]
        )
        for n in range(len(pieces))
    ]
    for copy in copies:
        copy.start()
    if carried:
        carry_copy = pltpu.make_async_copy(
            gx_in, x_v.at[pl.ds(rows, GLOBAL_ROWS), :], in_sem.at[len(pieces)]
        )
        carry_copy.start()
        carry_copy.wait()
    for copy in copies:
        copy.wait()

    if not carried:
        gx_copy = pltpu.make_async_copy(
            x_v.at[pl.ds(pl.multiple_of(jnp.maximum(glob, 0), BLK), GLOBAL_ROWS), :],
            gx_hbm,
            gx_sem,
        )

        @pl.when(glob >= 0)
        def _():
            gx_copy.start()

    out_copies = []
    for tile in range(tiles):
        for n in range(TILE // BLK):
            start = pl.multiple_of(starts[4 * tile + n], BLK)

            def move(c, carry, n=n, start=start):
                cols = pl.ds(pl.multiple_of(c * 512, 512), 512)
                slots_v[n * BLK : (n + 1) * BLK, cols] = x_v[pl.ds(start, BLK), cols]
                return carry

            lax.fori_loop(0, WIDTH // 512, move, 0)

        def low_of():
            return lax.dot_general(
                w_down[pl.ds(first * RANK, count * RANK), :],
                slots_v[...],
                (((1,), (1,)), ((), ())),
                preferred_element_type=jnp.float32,
            ).astype(jnp.bfloat16)

        project_tile(
            first, count, low_of, lambda cols: slots_v[:, cols], w_in, w_out, mid, out_v.at[tile]
        )
        for p in range(count):
            if first + p == 0:
                src, dst = out_v.at[tile, p, pl.ds(0, SHARD), :], q_hbm
            else:
                src = out_v.at[tile, p]
                dst = kv_hbm.at[first + p - 1, pl.ds(row0 + tile * TILE, TILE), :]
            copy = pltpu.make_async_copy(src, dst, out_sem.at[tile, p])
            copy.start()
            out_copies.append(copy)

    if with_own:

        def own_step(i, carry):
            span = pl.ds(pl.multiple_of(i * GTILE, GTILE), GTILE)
            own_v[span, :] = own_keys_values(x_v, span, own_in, own_out)
            return carry

        lax.fori_loop(0, rows // GTILE, own_step, 0)
        own_copy = pltpu.make_async_copy(own_v, own_hbm.at[pl.ds(own0, rows), :], own_sem)
        own_copy.start()
        own_copy.wait()
    for copy in out_copies:
        copy.wait()
    if not carried:

        @pl.when(glob >= 0)
        def _():
            gx_copy.wait()


def gather_step(kind, info, pieces, weights, own_weights, row0, own0, tiles, mode, previous):
    count = len(pieces)
    sizes = tuple(piece.shape[0] for piece in pieces)
    rows = sum(sizes) // GTILE * GTILE
    any_spec = pl.BlockSpec(memory_space=pl.ANY)
    vmem = pl.BlockSpec(memory_space=pltpu.VMEM)
    operands = list(pieces) + list(weights) + (list(own_weights) if mode == "both" else [])
    in_specs = [any_spec] * count + [vmem] * (len(operands) - count)
    out_shape = [jax.ShapeDtypeStruct((2, KV_ROWS, WIDTH), jnp.bfloat16)]
    if mode == "both":
        out_shape.append(jax.ShapeDtypeStruct((DOC, 2 * OWN_COLS), jnp.bfloat16))
    if mode == "query":
        out_shape.append(jax.ShapeDtypeStruct((SHARD, WIDTH), jnp.bfloat16))
    if mode != "slots":
        out_shape.append(jax.ShapeDtypeStruct((GLOBAL_ROWS, WIDTH), jnp.bfloat16))
    aliases = {}
    for value, out in previous:
        if out is not None:
            aliases[1 + len(operands)] = out
        operands.append(value)
        in_specs.append(any_spec)
    projections = 3 if mode == "query" else 2
    own_rows = rows if mode == "both" else 16
    return pl.pallas_call(
        functools.partial(step_body, kind, sizes, tiles, mode, row0, own0, len(previous)),
        out_shape=tuple(out_shape),
        grid_spec=pltpu.PrefetchScalarGridSpec(
            num_scalar_prefetch=1,
            grid=(),
            in_specs=in_specs,
            out_specs=(any_spec,) * len(out_shape),
            scratch_shapes=[
                pltpu.VMEM(
                    (sum(sizes) + (GLOBAL_ROWS if mode == "slots" else 0), WIDTH), jnp.bfloat16
                ),
                pltpu.VMEM((TILE, WIDTH), jnp.bfloat16),
                pltpu.VMEM((TILE // 128, projections * MB * PITCH, 128), jnp.float32),
                pltpu.VMEM((tiles, projections, TILE, WIDTH), jnp.bfloat16),
                pltpu.VMEM((own_rows, 2 * OWN_COLS), jnp.bfloat16),
                pltpu.SemaphoreType.DMA((count + 1,)),
                pltpu.SemaphoreType.DMA((tiles, projections)),
                pltpu.SemaphoreType.DMA(()),
                pltpu.SemaphoreType.DMA(()),
            ],
        ),
        input_output_aliases=aliases,
        compiler_params=pltpu.CompilerParams(vmem_limit_bytes=46 * 1024 * 1024),
        cost_estimate=pl.CostEstimate(
            flops=tiles * 8 * 10**9, bytes_accessed=20 * 10**6, transcendentals=0
        ),
        name="gather_step",
    )(info, *operands)


def far_body(own0, info, x0, x1, own_in, own_out, own_old, gx_old, own_hbm, gx_hbm, x_v, own_v, in_sem, out_sem):
    copies = [
        pltpu.make_async_copy(x, x_v.at[pl.ds(n * SHARD, SHARD), :], in_sem.at[n])
        for n, x in enumerate((x0, x1))
    ]
    for copy in copies:
        copy.start()
    for copy in copies:
        copy.wait()
    _, glob = step_rows(info, CHIPS // 2, 2)
    gx_copy = pltpu.make_async_copy(
        x_v.at[pl.ds(pl.multiple_of(jnp.maximum(glob, 0), BLK), GLOBAL_ROWS), :],
        gx_hbm,
        out_sem.at[0],
    )

    @pl.when(glob >= 0)
    def _():
        gx_copy.start()

    own_v[...] = own_keys_values(x_v, slice(0, GTILE), own_in, own_out)
    own_copy = pltpu.make_async_copy(own_v, own_hbm.at[pl.ds(own0, GTILE), :], out_sem.at[1])
    own_copy.start()
    own_copy.wait()

    @pl.when(glob >= 0)
    def _():
        gx_copy.wait()


def far_own(info, pieces, own_weights, own_kv, gx, own0):
    any_spec = pl.BlockSpec(memory_space=pl.ANY)
    vmem = pl.BlockSpec(memory_space=pltpu.VMEM)
    return pl.pallas_call(
        functools.partial(far_body, own0),
        out_shape=(
            jax.ShapeDtypeStruct(own_kv.shape, own_kv.dtype),
            jax.ShapeDtypeStruct(gx.shape, gx.dtype),
        ),
        in_specs=[pl.BlockSpec(memory_space=pltpu.SMEM), any_spec, any_spec, vmem, vmem]
        + [any_spec] * 2,
        out_specs=(any_spec, any_spec),
        scratch_shapes=[
            pltpu.VMEM((GTILE, WIDTH), jnp.bfloat16),
            pltpu.VMEM((GTILE, 2 * OWN_COLS), jnp.bfloat16),
            pltpu.SemaphoreType.DMA((2,)),
            pltpu.SemaphoreType.DMA((2,)),
        ],
        input_output_aliases={5: 0, 6: 1},
        compiler_params=pltpu.CompilerParams(vmem_limit_bytes=46 * 1024 * 1024),
        cost_estimate=pl.CostEstimate(
            flops=2 * 10**9, bytes_accessed=6 * 10**6, transcendentals=0
        ),
        name="far_own",
    )(info, *pieces, *own_weights, own_kv, gx)


KEY_SLOTS = GLOB_BLOCKS + 2 + LOCAL_BLOCKS + LOCAL_BLOCKS * RAND
WINDOW_ROW = GLOB_BLOCKS * BLK
RANDOM_ROW = WINDOW_ROW + (LOCAL_BLOCKS + 2) * BLK
LOCAL_COLS = 1024
EXP_SCALE = float(HD) ** -0.5 * 1.4426950408889634


def softmax_mix(queries, keys, values, biases):
    scores = []
    for q, k, bias in zip(queries, keys, biases):
        score = lax.dot_general(
            q, k(), (((1,), (1,)), ((), ())), preferred_element_type=jnp.float32
        )
        scores.append(score if bias is None else score + bias)
    peaks = [jnp.max(score, axis=-1, keepdims=True) * EXP_SCALE for score in scores]
    weights = [jnp.exp2(score * EXP_SCALE - peak) for score, peak in zip(scores, peaks)]
    totals = [jnp.sum(weight, axis=-1, keepdims=True) for weight in weights]
    numers = [
        jnp.dot(weight.astype(jnp.bfloat16), v(), preferred_element_type=jnp.float32)
        for weight, v in zip(weights, values)
    ]
    return [
        (numer * (1.0 / total)).astype(jnp.bfloat16) for numer, total in zip(numers, totals)
    ]


def random_block(info, r):
    named, seq = info[1 + r], info[0]
    source = lax.div(named, LOCAL_BLOCKS)
    distance = lax.rem(lax.div(source, 2) - lax.div(seq, 2) + CHIPS, CHIPS)
    other = lax.rem(source + seq, 2)
    ahead = jnp.where(distance < CHIPS // 2, 1, 0)
    step = jnp.where(ahead == 1, distance, CHIPS - distance)
    place = 4 * step + jnp.where(step == 3, 4, 0) + 2 * other + ahead
    place = jnp.where(step == CHIPS // 2, FAR_SLOT + other, place)
    place = jnp.where(distance == 0, PARTNER_SLOT, place)
    return jnp.where(source == seq, lax.rem(named, LOCAL_BLOCKS), place)


def local_body(group, info, q_hbm, kv_hbm, out_ref, q_v, held, sem):
    core = lax.rem(info[0], 2)
    below = jnp.where(core == 0, EDGE_FAR, EDGE_NEAR)
    above = jnp.where(core == 0, EDGE_NEAR, EDGE_FAR)
    runs = [(GLOBAL_SLOT, 0, 2), (below, 2, 1), (0, 3, LOCAL_BLOCKS), (above, 6, 1)]
    runs += [(random_block(info, r), 7 + r, 1) for r in range(LOCAL_BLOCKS * RAND)]
    sides = 2
    half = LOCAL_COLS // sides
    q_copy = pltpu.make_async_copy(
        q_hbm.at[:, pl.ds(group * LOCAL_COLS, LOCAL_COLS)], q_v, sem.at[sides, 0]
    )
    q_copy.start()
    copies = []
    for side in range(sides):
        cols = pl.ds(group * LOCAL_COLS + side * half, half)
        for n, (source, target, count) in enumerate(runs):
            rows = pl.ds(pl.multiple_of(source * BLK, BLK), count * BLK)
            copies.append(
                pltpu.make_async_copy(
                    kv_hbm.at[:, rows, cols],
                    held.at[side, :, pl.ds(target * BLK, count * BLK), :],
                    sem.at[side, n],
                )
            )
    for copy in copies:
        copy.start()
    lane = lax.broadcasted_iota(jnp.int32, (1, 8 * BLK), 1)
    biases = []
    for b in range(LOCAL_BLOCKS):
        block = info[0] * LOCAL_BLOCKS + b
        blocked = ((lane >= 128) & (lane < 192) & (block - 1 < GLOB_BLOCKS)) | (
            (lane >= 256) & (lane < 320) & (block + 1 >= DOC // BLK)
        )
        biases.append(jnp.where(blocked, -jnp.inf, 0.0))
    q_copy.wait()
    for side in range(sides):
        for copy in copies[side * len(runs) : (side + 1) * len(runs)]:
            copy.wait()
        units = [(h, b) for h in range(half // HD) for b in range(LOCAL_BLOCKS)]

        def block_rows(plane, h, b, side=side):
            cols = slice(h * HD, (h + 1) * HD)
            first = WINDOW_ROW + b * BLK
            second = RANDOM_ROW + b * RAND * BLK
            return jnp.concatenate(
                [
                    held[side, plane, 0:WINDOW_ROW, cols],
                    held[side, plane, first : first + 3 * BLK, cols],
                    held[side, plane, second : second + RAND * BLK, cols],
                ],
                axis=0,
            )

        def places(h, b, side=side):
            return slice(b * BLK, (b + 1) * BLK), slice(
                side * half + h * HD, side * half + (h + 1) * HD
            )

        mixed = softmax_mix(
            [q_v[places(h, b)] for h, b in units],
            [functools.partial(block_rows, 0, h, b) for h, b in units],
            [functools.partial(block_rows, 1, h, b) for h, b in units],
            [biases[b] for _, b in units],
        )
        for (h, b), rows in zip(units, mixed):
            out_ref[places(h, b)] = rows


def attend_local(group, info, q, kv):
    any_spec = pl.BlockSpec(memory_space=pl.ANY)
    return pl.pallas_call(
        functools.partial(local_body, group),
        out_shape=jax.ShapeDtypeStruct((SHARD, LOCAL_COLS), jnp.bfloat16),
        in_specs=[pl.BlockSpec(memory_space=pltpu.SMEM), any_spec, any_spec],
        out_specs=pl.BlockSpec(memory_space=pltpu.VMEM),
        scratch_shapes=[
            pltpu.VMEM((SHARD, LOCAL_COLS), jnp.bfloat16),
            pltpu.VMEM((2, 2, KEY_SLOTS * BLK, LOCAL_COLS // 2), jnp.bfloat16),
            pltpu.SemaphoreType.DMA((3, 4 + LOCAL_BLOCKS * RAND)),
        ],
        compiler_params=pltpu.CompilerParams(vmem_limit_bytes=48 * 1024 * 1024),
        cost_estimate=pl.CostEstimate(
            flops=4 * 10**9, bytes_accessed=5 * 10**6, transcendentals=800000
        ),
        name="attend_local",
    )(info, q, kv)


def global_body(gx, own_in, own_out, w_down, kv_ref, out_ref):
    q = own_query(gx[...], own_in, own_out, w_down)
    heads = [slice(h * HD, (h + 1) * HD) for h in range(OWN_COLS // HD)]
    mixed = softmax_mix(
        [q[:, cols] for cols in heads],
        [lambda cols=cols: kv_ref[:, cols] for cols in heads],
        [lambda cols=cols: kv_ref[:, cols.start + OWN_COLS : cols.stop + OWN_COLS] for cols in heads],
        [None] * len(heads),
    )
    for cols, rows in zip(heads, mixed):
        out_ref[:, cols] = rows


def attend_global(gx, own_query_weights, w_down, own_kv):
    return pl.pallas_call(
        global_body,
        out_shape=jax.ShapeDtypeStruct((GLOBAL_ROWS, OWN_COLS), jnp.bfloat16),
        in_specs=[pl.BlockSpec(memory_space=pltpu.VMEM)] * 5,
        out_specs=pl.BlockSpec(memory_space=pltpu.VMEM),
        compiler_params=pltpu.CompilerParams(vmem_limit_bytes=40 * 1024 * 1024),
        cost_estimate=pl.CostEstimate(
            flops=2 * 10**9, bytes_accessed=8 * 10**6, transcendentals=800000
        ),
        name="attend_global",
    )(gx, *own_query_weights, w_down, own_kv)


def merge_body(info, head, *refs):
    out_ref = refs[-1]
    for group, part in enumerate(refs[:-1]):
        out_ref[:, group * LOCAL_COLS : (group + 1) * LOCAL_COLS] = part[...]

    @pl.when(info[0] == 0)
    def _():
        out_ref[0:GLOBAL_ROWS, :] = head[...]


def merge(info, head, parts):
    return pl.pallas_call(
        merge_body,
        out_shape=jax.ShapeDtypeStruct((SHARD, WIDTH), jnp.bfloat16),
        in_specs=[pl.BlockSpec(memory_space=pltpu.SMEM)]
        + [pl.BlockSpec(memory_space=pltpu.VMEM)] * (1 + len(parts)),
        out_specs=pl.BlockSpec(memory_space=pltpu.VMEM),
        compiler_params=pltpu.CompilerParams(vmem_limit_bytes=40 * 1024 * 1024),
        name="merge",
    )(info, head, *parts)


def main_body(inner, outer, up, w_in, w_out):
    row = lax.broadcasted_iota(jnp.int32, (MB, MB), 0)
    col = lax.broadcasted_iota(jnp.int32, (MB, MB), 1)
    unit = jnp.where(row == col, 1.0, 0.0).astype(jnp.bfloat16)
    lane = lax.broadcasted_iota(jnp.int32, (MB, 2 * MB), 1)
    zero = jnp.zeros((MB, MB), jnp.bfloat16)

    def pair(n, carry):
        p, g = n // PAIRS, n % PAIRS
        blocks = jnp.concatenate([inner[p, 2 * g], inner[p, 2 * g + 1]], axis=0)
        turned = lax.dot_general(
            unit, blocks, (((1,), (1,)), ((), ())), preferred_element_type=jnp.float32
        )
        w_in[p, g, 0:MB, :] = jnp.where(lane < MB, turned, 0.0).astype(jnp.bfloat16)
        w_in[p, g, MB : 2 * MB, :] = jnp.where(lane < MB, 0.0, turned).astype(jnp.bfloat16)
        w_out[p, g, 0:MB, :] = jnp.concatenate([outer[p, 2 * g], zero], axis=1)
        w_out[p, g, MB : 2 * MB, :] = jnp.concatenate([zero, outer[p, 2 * g + 1]], axis=1)
        cols = pl.ds(pl.multiple_of(g * HD, HD), HD)
        w_out[p, g, 2 * MB : 2 * MB + RANK, :] = up[p, :, cols]
        return carry

    lax.fori_loop(0, 3 * PAIRS, pair, 0, unroll=8)


def prepare_weights(inner, outer, down, up):
    vmem = pl.BlockSpec(memory_space=pltpu.VMEM)
    w_in, w_out = pl.pallas_call(
        main_body,
        out_shape=(
            jax.ShapeDtypeStruct((3, PAIRS, 2 * MB, 2 * MB), jnp.bfloat16),
            jax.ShapeDtypeStruct((3, PAIRS, 2 * MB + RANK, HD), jnp.bfloat16),
        ),
        in_specs=[vmem] * 3,
        out_specs=(vmem, vmem),
        compiler_params=pltpu.CompilerParams(vmem_limit_bytes=40 * 1024 * 1024),
        cost_estimate=pl.CostEstimate(flops=10**9, bytes_accessed=12 * 10**6, transcendentals=0),
        name="main_weights",
    )(inner, outer, up)
    return w_in, w_out, jnp.transpose(down, (0, 2, 1)).reshape(3 * RANK, WIDTH)


def own_body(info, inner, outer, up, w_down, q_in, q_out, kv_in, kv_out):
    own_j = OWN_COLS // MB
    col = lax.broadcasted_iota(jnp.int32, (MB, OWN_COLS), 1)
    row = lax.broadcasted_iota(jnp.int32, (MB, OWN_COLS), 0)
    pick = jnp.where(row == info[0] * own_j + col // MB, 1.0, 0.0).astype(jnp.bfloat16)
    col2 = lax.broadcasted_iota(jnp.int32, (MB, 128), 1)
    row2 = lax.broadcasted_iota(jnp.int32, (MB, 128), 0)
    near = row2 == info[0] * own_j + col2 % own_j
    pick_k = jnp.where(near & (col2 % 8 < own_j), 1.0, 0.0).astype(jnp.bfloat16)
    pick_v = jnp.where(near & (col2 % 8 >= own_j), 1.0, 0.0).astype(jnp.bfloat16)
    unit = jnp.where(
        lax.broadcasted_iota(jnp.int32, (2 * RANK, 128), 0)
        == lax.broadcasted_iota(jnp.int32, (2 * RANK, 128), 1),
        1.0,
        0.0,
    ).astype(jnp.bfloat16)
    own_cols = pl.ds(pl.multiple_of(info[0] * OWN_COLS, OWN_COLS), OWN_COLS)
    span = 512
    wide_col = lax.broadcasted_iota(jnp.int32, (span, OWN_COLS), 1) % MB
    wide_row = lax.broadcasted_iota(jnp.int32, (span, OWN_COLS), 0) // MB
    low_col = lax.broadcasted_iota(jnp.int32, (span, 128), 1) // 8
    low_row = lax.broadcasted_iota(jnp.int32, (span, 128), 0) // MB

    def fill(i, carry):
        rows = pl.ds(pl.multiple_of(i * span, span), span)
        first = i * (span // MB)
        picked = jnp.dot(inner[0, rows, :], pick, preferred_element_type=jnp.float32)
        q_in[rows, :] = jnp.where(wide_col == wide_row + first, picked, 0.0).astype(jnp.bfloat16)
        picked = jnp.dot(inner[1, rows, :], pick_k, preferred_element_type=jnp.float32)
        picked += jnp.dot(inner[2, rows, :], pick_v, preferred_element_type=jnp.float32)
        here = low_col == low_row + first % 16
        kv_in[rows, 0:128] = jnp.where(here, picked, 0.0).astype(jnp.bfloat16)
        turned = lax.dot_general(
            w_down[RANK : 3 * RANK, rows],
            unit,
            (((0,), (0,)), ((), ())),
            preferred_element_type=jnp.float32,
        )
        kv_in[rows, 128:256] = turned.astype(jnp.bfloat16)
        return carry

    lax.fori_loop(0, WIDTH // span, fill, 0)
    q_out[...] = jnp.zeros_like(q_out)
    kv_out[...] = jnp.zeros_like(kv_out)
    tall_row = lax.broadcasted_iota(jnp.int32, (2 * OWN_COLS, MB), 0)
    tall_col = lax.broadcasted_iota(jnp.int32, (2 * OWN_COLS, MB), 1)
    for j in range(own_j):
        q_out[j * MB : (j + 1) * MB, j * MB : (j + 1) * MB] = outer[0, info[0] * own_j + j]
        for p in range(2):
            place = jnp.where(tall_row == tall_col * 8 + (p * own_j + j), 1.0, 0.0)
            at = p * OWN_COLS + j * MB
            kv_out[0 : 2 * OWN_COLS, at : at + MB] = jnp.dot(
                place.astype(jnp.bfloat16),
                outer[1 + p, info[0] * own_j + j],
                preferred_element_type=jnp.float32,
            ).astype(jnp.bfloat16)
    q_out[OWN_COLS : OWN_COLS + RANK, :] = up[0, :, own_cols]
    for p in range(2):
        at = 2 * OWN_COLS + p * RANK
        kv_out[at : at + RANK, p * OWN_COLS : (p + 1) * OWN_COLS] = up[1 + p, :, own_cols]


def own_head_weights(info, inner, outer, up, w_down):
    vmem = pl.BlockSpec(memory_space=pltpu.VMEM)
    shapes = (
        (WIDTH, OWN_COLS),
        (OWN_COLS + RANK, OWN_COLS),
        (WIDTH, 256),
        (2 * OWN_COLS + 128, 2 * OWN_COLS),
    )
    q_in, q_out, kv_in, kv_out = pl.pallas_call(
        own_body,
        out_shape=tuple(jax.ShapeDtypeStruct(shape, jnp.bfloat16) for shape in shapes),
        in_specs=[pl.BlockSpec(memory_space=pltpu.SMEM)] + [vmem] * 4,
        out_specs=(vmem,) * 4,
        compiler_params=pltpu.CompilerParams(vmem_limit_bytes=40 * 1024 * 1024),
        name="own_weights",
    )(info, inner.reshape(3, WIDTH, MB), outer, up, w_down)
    return (q_in, q_out), (kv_in, kv_out)


EDGE_NEAR, PARTNER_SLOT, EDGE_FAR, FAR_SLOT, GLOBAL_SLOT = 3, 12, 13, 20, 22


def shift(step):
    return [
        (z * 2 + c, ((z + step) % CHIPS) * 2 + c) for z in range(CHIPS) for c in range(2)
    ]


SWAP = [(i, i ^ 1) for i in range(2 * CHIPS)]
SPLIT = [
    (z * 2 + c, ((z + (1 if c == 0 else -1)) % CHIPS) * 2 + c)
    for z in range(CHIPS)
    for c in range(2)
]


def per_device(tokens, inner, outer, down, up, pattern):
    seq = lax.axis_index("seq").astype(jnp.int32)
    core = seq % 2
    mine = lax.dynamic_slice_in_dim(pattern, seq * LOCAL_BLOCKS, LOCAL_BLOCKS, 0).reshape(-1)
    info = jnp.concatenate([seq[None], mine]).astype(jnp.int32)

    def swap(value):
        return lax.ppermute(value, "seq", SWAP)

    def hop(forward, backward):
        return (
            lax.ppermute(forward, "seq", shift(1)),
            lax.ppermute(backward, "seq", shift(-1)),
        )

    partner = swap(tokens)
    forward, backward = hop(tokens, tokens)
    weights = prepare_weights(inner, outer, down, up)
    kv, q, gx = gather_step(0, info, (tokens, partner), weights, None, 0, 0, 1, "query", ())
    own_kv = None
    own0 = 0
    for step in range(1, CHIPS // 2):
        if own_kv is None:
            forward, backward, kv, gx, late = lax.optimization_barrier(
                (forward, backward, kv, gx, info)
            )
            own_query_weights, own_kv_weights = own_head_weights(late, inner, outer, up, weights[2])
        else:
            forward, backward, kv, gx, own_kv = lax.optimization_barrier(
                (forward, backward, kv, gx, own_kv)
            )
        pieces = (forward, backward, swap(forward), swap(backward))
        tiles = 1
        if step == 1:
            edge = jnp.where(core == 0, pieces[2][2 * BLK :], pieces[3][:BLK])
        if step == 2:
            tiles = 2
            pieces += (partner, tokens, edge)
        if step < CHIPS // 2 - 1:
            forward, backward = hop(forward, backward)
        else:
            far = lax.ppermute(jnp.where(core == 0, forward, backward), "seq", SPLIT)
        previous = [(kv, 0)] + ([(own_kv, 1)] if own_kv is not None else []) + [(gx, 2)]
        row0 = {1: 4, 2: 8, 3: 16}[step] * BLK
        kv, own_kv, gx = gather_step(
            step, info, pieces, weights, own_kv_weights, row0, own0, tiles, "both", previous
        )
        own0 += len(pieces[:6]) * SHARD
    far, kv, own_kv, gx = lax.optimization_barrier((far, kv, own_kv, gx))
    far_pieces = (far, swap(far))
    own_kv, gx = far_own(info, far_pieces, own_kv_weights, own_kv, gx, own0)

    head = attend_global(gx, own_query_weights, weights[2], own_kv)
    sent = lax.ppermute(head, "seq", [(i + 1, i) for i in range(0, 2 * CHIPS, 2)])
    gx, head = lax.optimization_barrier((gx, head))
    (kv,) = gather_step(
        CHIPS // 2,
        info,
        far_pieces,
        weights,
        None,
        20 * BLK,
        0,
        1,
        "slots",
        [(kv, 0), (gx, None)],
    )
    head = jnp.concatenate([head, sent], axis=1)
    parts = []
    reach = 2
    for group in range(WIDTH // LOCAL_COLS):
        if reach < 2 * CHIPS:
            pairs = [(i + reach, i) for i in range(0, 2 * CHIPS, 2 * reach)]
            sent = lax.ppermute(head, "seq", pairs)
            kv, head = lax.optimization_barrier((kv, head))
        parts.append(attend_local(group, info, q, kv))
        if reach < 2 * CHIPS:
            head = jnp.concatenate([head, sent], axis=1)
        reach *= 2
    return merge(info, head, parts)


def solution(mesh):
    return jax.shard_map(
        per_device,
        mesh=mesh,
        in_specs=(P(("dp", "seq"), None), P(), P(), P(), P(), P("dp", None)),
        out_specs=P(("dp", "seq"), None),
        check_vma=False,
    )
```

```python
import functools

import jax
import jax.numpy as jnp
from jax import lax
from jax.experimental import pallas as pl
from jax.experimental.pallas import tpu as pltpu
from jax.sharding import PartitionSpec as P

HEADS = 32
HD = 128
BLK = 64
RAND = 3
GLOB_BLOCKS = 2
WIDTH = 4096
MB = 64
RANK = 16
TILE = 256
GTILE = 384
GROUP_IN = 8
GROUP_OUT = 4
PAIRS = MB // 2
CHIPS = 8
LOCAL_BLOCKS = 3
SHARD = LOCAL_BLOCKS * BLK
DOC = 3072
PITCH = 72
GLOBAL_ROWS = GLOB_BLOCKS * BLK
OWN_COLS = WIDTH // (2 * CHIPS)
KV_ROWS = 1536


def project_tile(first, count, low_of, x_of, w_in, w_out, mid, out_v):
    low = low_of()
    group_in = GROUP_IN * (2 if count == 1 else 1)
    group_out = GROUP_OUT * (2 if count == 1 else 1)

    def inner_step(i, carry):
        made = []
        for n in range(group_in):
            g = i * group_in + n
            xg = x_of(pl.ds(pl.multiple_of(g * 128, 128), 128))
            for p in range(count):
                part = lax.dot_general(
                    w_in[first + p, g],
                    xg,
                    (((1,), (1,)), ((), ())),
                    preferred_element_type=jnp.float32,
                )
                made.append((g, p, part))
        for g, p, part in made:
            for a in range(2):
                start = pl.multiple_of((p * MB + 2 * g + a) * PITCH, 8)
                for lanes in range(TILE // 128):
                    mid[lanes, pl.ds(start, MB), :] = part[
                        a * MB : (a + 1) * MB, lanes * 128 : (lanes + 1) * 128
                    ]
        return carry

    lax.fori_loop(0, PAIRS // group_in, inner_step, 0)

    def outer_step(i, carry):
        units = [(i * group_out + n, p) for n in range(group_out) for p in range(count)]
        stacks = []
        for h, p in units:
            base = p * MB * PITCH + 2 * h
            parts = []
            for lanes in range(TILE // 128):
                one = mid[lanes, pl.ds(base, MB, stride=PITCH), :]
                two = mid[lanes, pl.ds(base + 1, MB, stride=PITCH), :]
                parts.append(
                    jnp.concatenate([one.astype(jnp.bfloat16), two.astype(jnp.bfloat16)], axis=0)
                )
            stacks.append(
                jnp.concatenate(
                    [jnp.concatenate(parts, axis=1), low[p * RANK : (p + 1) * RANK]], axis=0
                )
            )
        made = [
            lax.dot_general(
                stack,
                w_out[first + p, h],
                (((0,), (0,)), ((), ())),
                preferred_element_type=jnp.float32,
            )
            for stack, (h, p) in zip(stacks, units)
        ]
        for done, (h, p) in zip(made, units):
            out_v[p, :, pl.ds(pl.multiple_of(h * 128, 128), 128)] = done.astype(jnp.bfloat16)
        return carry

    lax.fori_loop(0, HEADS // group_out, outer_step, 0)


def named_block(info, source):
    block = jnp.int32(0)
    for r in range(LOCAL_BLOCKS * RAND):
        named = info[1 + r]
        block = jnp.where(lax.div(named, LOCAL_BLOCKS) == source, lax.rem(named, LOCAL_BLOCKS), block)
    return block


def source_of(info, offset):
    dz, cls = offset
    chip = lax.rem(lax.div(info[0], 2) + (dz + CHIPS), CHIPS)
    return chip * 2 + lax.rem(info[0] + cls, 2)


def step_rows(info, kind, pieces):
    core = lax.rem(info[0], 2)
    if kind == 0:
        near = SHARD + jnp.where(core == 0, 0, 2 * BLK)
        glob = jnp.where(info[0] == 0, 0, jnp.where(info[0] == 1, SHARD, -1))
        return [0, BLK, 2 * BLK, near], glob
    if kind == CHIPS // 2:
        offsets = [(kind, 0), (kind, 1)]
    else:
        offsets = [(-kind, 0), (kind, 0), (-kind, 1), (kind, 1)]
    starts = []
    glob = jnp.int32(-1)
    for n, offset in enumerate(offsets):
        source = source_of(info, offset)
        starts.append(n * SHARD + BLK * named_block(info, source))
        glob = jnp.where(source == 0, n * SHARD, glob)
    if kind == 2:
        partner = info[0] + 1 - 2 * core
        starts += [4 * SHARD + BLK * named_block(info, partner), 6 * SHARD, 0, 0]
    return starts, glob


def own_query(x, own_in, own_out, w_down):
    inner = jnp.dot(x, own_in[...], preferred_element_type=jnp.float32)
    low = lax.dot_general(
        x, w_down[0:RANK, :], (((1,), (1,)), ((), ())), preferred_element_type=jnp.float32
    )
    main = jnp.dot(
        inner.astype(jnp.bfloat16), own_out[0:OWN_COLS, :], preferred_element_type=jnp.float32
    )
    lifted = jnp.dot(
        low.astype(jnp.bfloat16), own_out[OWN_COLS:, :], preferred_element_type=jnp.float32
    )
    return (main + lifted).astype(jnp.bfloat16)


def own_keys_values(x_v, span, own_in, own_out):
    quarter = WIDTH // 4
    parts, low = [], None
    for n in range(4):
        cols = slice(n * quarter, (n + 1) * quarter)
        part = jnp.dot(x_v[span, cols], own_in[cols, :], preferred_element_type=jnp.float32)
        parts.append(part[:, 0:128].astype(jnp.bfloat16))
        low = part[:, 128:256] if low is None else low + part[:, 128:256]
    parts.append(low.astype(jnp.bfloat16))
    inner = jnp.concatenate(parts, axis=1)
    return jnp.dot(inner, own_out[...], preferred_element_type=jnp.float32).astype(jnp.bfloat16)


def step_body(kind, pieces, tiles, mode, row0, own0, alias, info, *refs):
    x_hbm = refs[: len(pieces)]
    at = len(pieces)
    with_own, carried = mode == "both", mode in ("keys", "values")
    w_in, w_out, w_down = refs[at : at + 3]
    at += 3
    if with_own:
        own_in, own_out = refs[at : at + 2]
        at += 2
    gx_in = refs[at + alias - 1] if alias else None
    at += alias
    kv_hbm = refs[at]
    at += 1
    if with_own:
        own_hbm = refs[at]
        at += 1
    if mode == "query":
        q_hbm = refs[at]
        at += 1
    if not carried:
        gx_hbm = refs[at]
        at += 1
    x_v, slots_v, mid, out_v, own_v, in_sem, out_sem, own_sem, gx_sem = refs[at:]
    rows = sum(pieces) // GTILE * GTILE
    first, count = PROJECTIONS[mode]
    starts, glob = step_rows(info, kind, len(pieces))

    if carried:
        copies = [
            pltpu.make_async_copy(
                x_hbm[n].at[pl.ds(pl.multiple_of(starts[n] - n * SHARD, BLK), BLK), :],
                slots_v.at[pl.ds(n * BLK, BLK), :],
                in_sem.at[n],
            )
            for n in range(len(pieces))
        ]
        copies.append(
            pltpu.make_async_copy(
                gx_in,
                slots_v.at[pl.ds(len(pieces) * BLK, GLOBAL_ROWS), :],
                in_sem.at[len(pieces)],
            )
        )
    else:
        copies = [
            pltpu.make_async_copy(
                x_hbm[n], x_v.at[pl.ds(n * SHARD, pieces[n]), :], in_sem.at[n]
            )
            for n in range(len(pieces))
        ]
    for copy in copies:
        copy.start()
    for copy in copies:
        copy.wait()

    if not carried:
        gx_copy = pltpu.make_async_copy(
            x_v.at[pl.ds(pl.multiple_of(jnp.maximum(glob, 0), BLK), GLOBAL_ROWS), :],
            gx_hbm,
            gx_sem,
        )

        @pl.when(glob >= 0)
        def _():
            gx_copy.start()

    out_copies = []
    for tile in range(tiles):
        for n in range(0 if carried else TILE // BLK):
            start = pl.multiple_of(starts[4 * tile + n], BLK)

            def move(c, carry, n=n, start=start):
                cols = pl.ds(pl.multiple_of(c * 512, 512), 512)
                slots_v[n * BLK : (n + 1) * BLK, cols] = x_v[pl.ds(start, BLK), cols]
                return carry

            lax.fori_loop(0, WIDTH // 512, move, 0)

        def low_of():
            return lax.dot_general(
                w_down[pl.ds(first * RANK, count * RANK), :],
                slots_v[...],
                (((1,), (1,)), ((), ())),
                preferred_element_type=jnp.float32,
            ).astype(jnp.bfloat16)

        project_tile(
            first, count, low_of, lambda cols: slots_v[:, cols], w_in, w_out, mid, out_v.at[tile]
        )
        for p in range(count):
            if first + p == 0:
                src, dst = out_v.at[tile, p, pl.ds(0, SHARD), :], q_hbm
            else:
                src = out_v.at[tile, p]
                dst = kv_hbm.at[first + p - 1, pl.ds(row0 + tile * TILE, TILE), :]
            copy = pltpu.make_async_copy(src, dst, out_sem.at[tile, p])
            copy.start()
            out_copies.append(copy)

    if with_own:

        def own_step(i, carry):
            span = pl.ds(pl.multiple_of(i * GTILE, GTILE), GTILE)
            own_v[span, :] = own_keys_values(x_v, span, own_in, own_out)
            return carry

        lax.fori_loop(0, rows // GTILE, own_step, 0)
        own_copy = pltpu.make_async_copy(own_v, own_hbm.at[pl.ds(own0, rows), :], own_sem)
        own_copy.start()
        own_copy.wait()
    for copy in out_copies:
        copy.wait()
    if not carried:

        @pl.when(glob >= 0)
        def _():
            gx_copy.wait()


PROJECTIONS = {"query": (0, 3), "both": (1, 2), "keys": (1, 1), "values": (2, 1)}


def gather_step(kind, info, pieces, weights, own_weights, row0, own0, tiles, mode, previous):
    count = len(pieces)
    sizes = tuple(piece.shape[0] for piece in pieces)
    rows = sum(sizes) // GTILE * GTILE
    any_spec = pl.BlockSpec(memory_space=pl.ANY)
    vmem = pl.BlockSpec(memory_space=pltpu.VMEM)
    operands = list(pieces) + list(weights) + (list(own_weights) if mode == "both" else [])
    in_specs = [any_spec] * count + [vmem] * (len(operands) - count)
    out_shape = [jax.ShapeDtypeStruct((2, KV_ROWS, WIDTH), jnp.bfloat16)]
    if mode == "both":
        out_shape.append(jax.ShapeDtypeStruct((DOC, 2 * OWN_COLS), jnp.bfloat16))
    if mode == "query":
        out_shape.append(jax.ShapeDtypeStruct((SHARD, WIDTH), jnp.bfloat16))
    if mode in ("query", "both"):
        out_shape.append(jax.ShapeDtypeStruct((GLOBAL_ROWS, WIDTH), jnp.bfloat16))
    aliases = {}
    for value, out in previous:
        if out is not None:
            aliases[1 + len(operands)] = out
        operands.append(value)
        in_specs.append(any_spec)
    projections = PROJECTIONS[mode][1]
    own_rows = rows if mode == "both" else 16
    return pl.pallas_call(
        functools.partial(step_body, kind, sizes, tiles, mode, row0, own0, len(previous)),
        out_shape=tuple(out_shape),
        grid_spec=pltpu.PrefetchScalarGridSpec(
            num_scalar_prefetch=1,
            grid=(),
            in_specs=in_specs,
            out_specs=(any_spec,) * len(out_shape),
            scratch_shapes=[
                pltpu.VMEM((sum(sizes) if mode in ("query", "both") else BLK, WIDTH), jnp.bfloat16),
                pltpu.VMEM((TILE, WIDTH), jnp.bfloat16),
                pltpu.VMEM((TILE // 128, projections * MB * PITCH, 128), jnp.float32),
                pltpu.VMEM((tiles, projections, TILE, WIDTH), jnp.bfloat16),
                pltpu.VMEM((own_rows, 2 * OWN_COLS), jnp.bfloat16),
                pltpu.SemaphoreType.DMA((count + 1,)),
                pltpu.SemaphoreType.DMA((tiles, projections)),
                pltpu.SemaphoreType.DMA(()),
                pltpu.SemaphoreType.DMA(()),
            ],
        ),
        input_output_aliases=aliases,
        compiler_params=pltpu.CompilerParams(vmem_limit_bytes=46 * 1024 * 1024),
        cost_estimate=pl.CostEstimate(
            flops=tiles * projections * 4 * 10**9, bytes_accessed=20 * 10**6, transcendentals=0
        ),
        name="gather_step",
    )(info, *operands)


KEY_SLOTS = GLOB_BLOCKS + 2 + LOCAL_BLOCKS + LOCAL_BLOCKS * RAND
WINDOW_ROW = GLOB_BLOCKS * BLK
RANDOM_ROW = WINDOW_ROW + (LOCAL_BLOCKS + 2) * BLK
SIDE_COLS = 512
EXP_SCALE = float(HD) ** -0.5 * 1.4426950408889634


def softmax_mix(queries, keys, values, biases):
    scores = []
    for q, k, bias in zip(queries, keys, biases):
        score = lax.dot_general(
            q, k(), (((1,), (1,)), ((), ())), preferred_element_type=jnp.float32
        )
        scores.append(score if bias is None else score + bias)
    peaks = [jnp.max(score, axis=-1, keepdims=True) * EXP_SCALE for score in scores]
    weights = [jnp.exp2(score * EXP_SCALE - peak) for score, peak in zip(scores, peaks)]
    totals = [jnp.sum(weight, axis=-1, keepdims=True) for weight in weights]
    numers = [
        jnp.dot(weight.astype(jnp.bfloat16), v(), preferred_element_type=jnp.float32)
        for weight, v in zip(weights, values)
    ]
    return [
        (numer * (1.0 / total)).astype(jnp.bfloat16) for numer, total in zip(numers, totals)
    ]


def random_block(info, r):
    named, seq = info[1 + r], info[0]
    source = lax.div(named, LOCAL_BLOCKS)
    distance = lax.rem(lax.div(source, 2) - lax.div(seq, 2) + CHIPS, CHIPS)
    other = lax.rem(source + seq, 2)
    ahead = jnp.where(distance < CHIPS // 2, 1, 0)
    step = jnp.where(ahead == 1, distance, CHIPS - distance)
    place = 4 * step + jnp.where(step == 3, 4, 0) + 2 * other + ahead
    place = jnp.where(step == CHIPS // 2, FAR_SLOT + other, place)
    place = jnp.where(distance == 0, PARTNER_SLOT, place)
    return jnp.where(source == seq, lax.rem(named, LOCAL_BLOCKS), place)


def local_body(col0, width, info, q_hbm, kv_hbm, out_ref, q_v, held, sem):
    core = lax.rem(info[0], 2)
    below = jnp.where(core == 0, EDGE_FAR, EDGE_NEAR)
    above = jnp.where(core == 0, EDGE_NEAR, EDGE_FAR)
    runs = [(GLOBAL_SLOT, 0, 2), (below, 2, 1), (0, 3, LOCAL_BLOCKS), (above, 6, 1)]
    runs += [(random_block(info, r), 7 + r, 1) for r in range(LOCAL_BLOCKS * RAND)]
    half = SIDE_COLS
    sides = width // half
    q_copy = pltpu.make_async_copy(q_hbm.at[:, pl.ds(col0, width)], q_v, sem.at[sides, 0])
    q_copy.start()
    copies = []
    for side in range(sides):
        cols = pl.ds(col0 + side * half, half)
        for n, (source, target, count) in enumerate(runs):
            rows = pl.ds(pl.multiple_of(source * BLK, BLK), count * BLK)
            copies.append(
                pltpu.make_async_copy(
                    kv_hbm.at[:, rows, cols],
                    held.at[side, :, pl.ds(target * BLK, count * BLK), :],
                    sem.at[side, n],
                )
            )
    for copy in copies:
        copy.start()
    lane = lax.broadcasted_iota(jnp.int32, (1, 8 * BLK), 1)
    biases = []
    for b in range(LOCAL_BLOCKS):
        block = info[0] * LOCAL_BLOCKS + b
        blocked = ((lane >= 128) & (lane < 192) & (block - 1 < GLOB_BLOCKS)) | (
            (lane >= 256) & (lane < 320) & (block + 1 >= DOC // BLK)
        )
        biases.append(jnp.where(blocked, -jnp.inf, 0.0))
    q_copy.wait()
    for side in range(sides):
        for copy in copies[side * len(runs) : (side + 1) * len(runs)]:
            copy.wait()
        units = [(h, b) for h in range(half // HD) for b in range(LOCAL_BLOCKS)]

        def block_rows(plane, h, b, side=side):
            cols = slice(h * HD, (h + 1) * HD)
            first = WINDOW_ROW + b * BLK
            second = RANDOM_ROW + b * RAND * BLK
            return jnp.concatenate(
                [
                    held[side, plane, 0:WINDOW_ROW, cols],
                    held[side, plane, first : first + 3 * BLK, cols],
                    held[side, plane, second : second + RAND * BLK, cols],
                ],
                axis=0,
            )

        def places(h, b, side=side):
            return slice(b * BLK, (b + 1) * BLK), slice(
                side * half + h * HD, side * half + (h + 1) * HD
            )

        mixed = softmax_mix(
            [q_v[places(h, b)] for h, b in units],
            [functools.partial(block_rows, 0, h, b) for h, b in units],
            [functools.partial(block_rows, 1, h, b) for h, b in units],
            [biases[b] for _, b in units],
        )
        for (h, b), rows in zip(units, mixed):
            out_ref[places(h, b)] = rows


def attend_local(col0, width, info, q, kv):
    any_spec = pl.BlockSpec(memory_space=pl.ANY)
    sides = width // SIDE_COLS
    return pl.pallas_call(
        functools.partial(local_body, col0, width),
        out_shape=jax.ShapeDtypeStruct((SHARD, width), jnp.bfloat16),
        in_specs=[pl.BlockSpec(memory_space=pltpu.SMEM), any_spec, any_spec],
        out_specs=pl.BlockSpec(memory_space=pltpu.VMEM),
        scratch_shapes=[
            pltpu.VMEM((SHARD, width), jnp.bfloat16),
            pltpu.VMEM((sides, 2, KEY_SLOTS * BLK, SIDE_COLS), jnp.bfloat16),
            pltpu.SemaphoreType.DMA((sides + 1, 4 + LOCAL_BLOCKS * RAND)),
        ],
        compiler_params=pltpu.CompilerParams(vmem_limit_bytes=48 * 1024 * 1024),
        cost_estimate=pl.CostEstimate(
            flops=4 * 10**6 * width, bytes_accessed=5 * 10**3 * width, transcendentals=800 * width
        ),
        name="attend_local",
    )(info, q, kv)


def global_body(
    info, x0, x1, own_in, own_out, w_down, own_hbm, gx_old, q_in_hbm, q_out_hbm,
    out_ref, gx_hbm, x_v, kv_v, gx_v, q_in, q_out, sem,
):
    _, glob = step_rows(info, CHIPS // 2, 2)
    known = DOC - GTILE
    x_copies = [
        pltpu.make_async_copy(x, x_v.at[pl.ds(n * SHARD, SHARD), :], sem.at[n])
        for n, x in enumerate((x0, x1))
    ]
    copies = [
        pltpu.make_async_copy(q_in_hbm, q_in, sem.at[2]),
        pltpu.make_async_copy(q_out_hbm, q_out, sem.at[3]),
        pltpu.make_async_copy(own_hbm.at[pl.ds(0, known), :], kv_v.at[pl.ds(0, known), :], sem.at[4]),
    ]
    old_copy = pltpu.make_async_copy(gx_old, gx_v, sem.at[5])
    new_copy = pltpu.make_async_copy(
        x_v.at[pl.ds(pl.multiple_of(jnp.maximum(glob, 0), BLK), GLOBAL_ROWS), :], gx_v, sem.at[5]
    )
    for copy in x_copies:
        copy.start()

    @pl.when(glob < 0)
    def _():
        old_copy.start()

    for copy in copies:
        copy.start()
    for copy in x_copies:
        copy.wait()

    @pl.when(glob >= 0)
    def _():
        new_copy.start()
        new_copy.wait()

    @pl.when(glob < 0)
    def _():
        old_copy.wait()

    gx_copy = pltpu.make_async_copy(gx_v, gx_hbm, sem.at[6])
    gx_copy.start()
    kv_v[pl.ds(known, GTILE), :] = own_keys_values(x_v, slice(0, GTILE), own_in, own_out)
    for copy in copies:
        copy.wait()
    q = own_query(gx_v[...], q_in, q_out, w_down)
    heads = [slice(h * HD, (h + 1) * HD) for h in range(OWN_COLS // HD)]
    mixed = softmax_mix(
        [q[:, cols] for cols in heads],
        [lambda cols=cols: kv_v[:, cols] for cols in heads],
        [lambda cols=cols: kv_v[:, cols.start + OWN_COLS : cols.stop + OWN_COLS] for cols in heads],
        [None] * len(heads),
    )
    for cols, rows in zip(heads, mixed):
        out_ref[:, cols] = rows
    gx_copy.wait()


def attend_global(info, pieces, own_weights, w_down, own_kv, gx, own_query_weights):
    any_spec = pl.BlockSpec(memory_space=pl.ANY)
    vmem = pl.BlockSpec(memory_space=pltpu.VMEM)
    return pl.pallas_call(
        global_body,
        out_shape=(
            jax.ShapeDtypeStruct((GLOBAL_ROWS, OWN_COLS), jnp.bfloat16),
            jax.ShapeDtypeStruct(gx.shape, gx.dtype),
        ),
        in_specs=[pl.BlockSpec(memory_space=pltpu.SMEM), any_spec, any_spec]
        + [vmem] * 3
        + [any_spec] * 4,
        out_specs=(vmem, any_spec),
        scratch_shapes=[
            pltpu.VMEM((GTILE, WIDTH), jnp.bfloat16),
            pltpu.VMEM((DOC, 2 * OWN_COLS), jnp.bfloat16),
            pltpu.VMEM((GLOBAL_ROWS, WIDTH), jnp.bfloat16),
            pltpu.VMEM((WIDTH, OWN_COLS), jnp.bfloat16),
            pltpu.VMEM((OWN_COLS + RANK, OWN_COLS), jnp.bfloat16),
            pltpu.SemaphoreType.DMA((7,)),
        ],
        compiler_params=pltpu.CompilerParams(vmem_limit_bytes=46 * 1024 * 1024),
        cost_estimate=pl.CostEstimate(
            flops=4 * 10**9, bytes_accessed=12 * 10**6, transcendentals=800000
        ),
        name="attend_global",
    )(info, *pieces, *own_weights, w_down, own_kv, gx, *own_query_weights)


def merge_body(heads, info, *refs):
    out_ref = refs[-1]
    at = 0
    for part in refs[heads:-1]:
        width = part.shape[1]
        out_ref[:, at : at + width] = part[...]
        at += width

    @pl.when(info[0] == 0)
    def _():
        at = 0
        for head in refs[:heads]:
            width = head.shape[1]
            out_ref[0:GLOBAL_ROWS, at : at + width] = head[...]
            at += width


def merge(info, heads, parts):
    return pl.pallas_call(
        functools.partial(merge_body, len(heads)),
        out_shape=jax.ShapeDtypeStruct((SHARD, WIDTH), jnp.bfloat16),
        in_specs=[pl.BlockSpec(memory_space=pltpu.SMEM)]
        + [pl.BlockSpec(memory_space=pltpu.VMEM)] * (len(heads) + len(parts)),
        out_specs=pl.BlockSpec(memory_space=pltpu.VMEM),
        compiler_params=pltpu.CompilerParams(vmem_limit_bytes=40 * 1024 * 1024),
        name="merge",
    )(info, *heads, *parts)


def main_body(inner, outer, up, w_in, w_out):
    row = lax.broadcasted_iota(jnp.int32, (MB, MB), 0)
    col = lax.broadcasted_iota(jnp.int32, (MB, MB), 1)
    unit = jnp.where(row == col, 1.0, 0.0).astype(jnp.bfloat16)
    lane = lax.broadcasted_iota(jnp.int32, (MB, 2 * MB), 1)
    zero = jnp.zeros((MB, MB), jnp.bfloat16)

    def pair(n, carry):
        p, g = n // PAIRS, n % PAIRS
        blocks = jnp.concatenate([inner[p, 2 * g], inner[p, 2 * g + 1]], axis=0)
        turned = lax.dot_general(
            unit, blocks, (((1,), (1,)), ((), ())), preferred_element_type=jnp.float32
        )
        w_in[p, g, 0:MB, :] = jnp.where(lane < MB, turned, 0.0).astype(jnp.bfloat16)
        w_in[p, g, MB : 2 * MB, :] = jnp.where(lane < MB, 0.0, turned).astype(jnp.bfloat16)
        w_out[p, g, 0:MB, :] = jnp.concatenate([outer[p, 2 * g], zero], axis=1)
        w_out[p, g, MB : 2 * MB, :] = jnp.concatenate([zero, outer[p, 2 * g + 1]], axis=1)
        cols = pl.ds(pl.multiple_of(g * HD, HD), HD)
        w_out[p, g, 2 * MB : 2 * MB + RANK, :] = up[p, :, cols]
        return carry

    lax.fori_loop(0, 3 * PAIRS, pair, 0, unroll=8)


def prepare_weights(inner, outer, down, up):
    vmem = pl.BlockSpec(memory_space=pltpu.VMEM)
    w_in, w_out = pl.pallas_call(
        main_body,
        out_shape=(
            jax.ShapeDtypeStruct((3, PAIRS, 2 * MB, 2 * MB), jnp.bfloat16),
            jax.ShapeDtypeStruct((3, PAIRS, 2 * MB + RANK, HD), jnp.bfloat16),
        ),
        in_specs=[vmem] * 3,
        out_specs=(vmem, vmem),
        compiler_params=pltpu.CompilerParams(vmem_limit_bytes=40 * 1024 * 1024),
        cost_estimate=pl.CostEstimate(flops=10**9, bytes_accessed=12 * 10**6, transcendentals=0),
        name="main_weights",
    )(inner, outer, up)
    return w_in, w_out, jnp.transpose(down, (0, 2, 1)).reshape(3 * RANK, WIDTH)


def own_body(info, inner, outer, up, w_down, q_in, q_out, kv_in, kv_out):
    own_j = OWN_COLS // MB
    col = lax.broadcasted_iota(jnp.int32, (MB, OWN_COLS), 1)
    row = lax.broadcasted_iota(jnp.int32, (MB, OWN_COLS), 0)
    pick = jnp.where(row == info[0] * own_j + col // MB, 1.0, 0.0).astype(jnp.bfloat16)
    col2 = lax.broadcasted_iota(jnp.int32, (MB, 128), 1)
    row2 = lax.broadcasted_iota(jnp.int32, (MB, 128), 0)
    near = row2 == info[0] * own_j + col2 % own_j
    pick_k = jnp.where(near & (col2 % 8 < own_j), 1.0, 0.0).astype(jnp.bfloat16)
    pick_v = jnp.where(near & (col2 % 8 >= own_j), 1.0, 0.0).astype(jnp.bfloat16)
    unit = jnp.where(
        lax.broadcasted_iota(jnp.int32, (2 * RANK, 128), 0)
        == lax.broadcasted_iota(jnp.int32, (2 * RANK, 128), 1),
        1.0,
        0.0,
    ).astype(jnp.bfloat16)
    own_cols = pl.ds(pl.multiple_of(info[0] * OWN_COLS, OWN_COLS), OWN_COLS)
    span = 512
    wide_col = lax.broadcasted_iota(jnp.int32, (span, OWN_COLS), 1) % MB
    wide_row = lax.broadcasted_iota(jnp.int32, (span, OWN_COLS), 0) // MB
    low_col = lax.broadcasted_iota(jnp.int32, (span, 128), 1) // 8
    low_row = lax.broadcasted_iota(jnp.int32, (span, 128), 0) // MB

    def fill(i, carry):
        rows = pl.ds(pl.multiple_of(i * span, span), span)
        first = i * (span // MB)
        picked = jnp.dot(inner[0, rows, :], pick, preferred_element_type=jnp.float32)
        q_in[rows, :] = jnp.where(wide_col == wide_row + first, picked, 0.0).astype(jnp.bfloat16)
        picked = jnp.dot(inner[1, rows, :], pick_k, preferred_element_type=jnp.float32)
        picked += jnp.dot(inner[2, rows, :], pick_v, preferred_element_type=jnp.float32)
        here = low_col == low_row + first % 16
        kv_in[rows, 0:128] = jnp.where(here, picked, 0.0).astype(jnp.bfloat16)
        turned = lax.dot_general(
            w_down[RANK : 3 * RANK, rows],
            unit,
            (((0,), (0,)), ((), ())),
            preferred_element_type=jnp.float32,
        )
        kv_in[rows, 128:256] = turned.astype(jnp.bfloat16)
        return carry

    lax.fori_loop(0, WIDTH // span, fill, 0)
    q_out[...] = jnp.zeros_like(q_out)
    kv_out[...] = jnp.zeros_like(kv_out)
    tall_row = lax.broadcasted_iota(jnp.int32, (2 * OWN_COLS, MB), 0)
    tall_col = lax.broadcasted_iota(jnp.int32, (2 * OWN_COLS, MB), 1)
    for j in range(own_j):
        q_out[j * MB : (j + 1) * MB, j * MB : (j + 1) * MB] = outer[0, info[0] * own_j + j]
        for p in range(2):
            place = jnp.where(tall_row == tall_col * 8 + (p * own_j + j), 1.0, 0.0)
            at = p * OWN_COLS + j * MB
            kv_out[0 : 2 * OWN_COLS, at : at + MB] = jnp.dot(
                place.astype(jnp.bfloat16),
                outer[1 + p, info[0] * own_j + j],
                preferred_element_type=jnp.float32,
            ).astype(jnp.bfloat16)
    q_out[OWN_COLS : OWN_COLS + RANK, :] = up[0, :, own_cols]
    for p in range(2):
        at = 2 * OWN_COLS + p * RANK
        kv_out[at : at + RANK, p * OWN_COLS : (p + 1) * OWN_COLS] = up[1 + p, :, own_cols]


def own_head_weights(info, inner, outer, up, w_down):
    vmem = pl.BlockSpec(memory_space=pltpu.VMEM)
    shapes = (
        (WIDTH, OWN_COLS),
        (OWN_COLS + RANK, OWN_COLS),
        (WIDTH, 256),
        (2 * OWN_COLS + 128, 2 * OWN_COLS),
    )
    q_in, q_out, kv_in, kv_out = pl.pallas_call(
        own_body,
        out_shape=tuple(jax.ShapeDtypeStruct(shape, jnp.bfloat16) for shape in shapes),
        in_specs=[pl.BlockSpec(memory_space=pltpu.SMEM)] + [vmem] * 4,
        out_specs=(vmem,) * 4,
        compiler_params=pltpu.CompilerParams(vmem_limit_bytes=40 * 1024 * 1024),
        name="own_weights",
    )(info, inner.reshape(3, WIDTH, MB), outer, up, w_down)
    return (q_in, q_out), (kv_in, kv_out)


EDGE_NEAR, PARTNER_SLOT, EDGE_FAR, FAR_SLOT, GLOBAL_SLOT = 3, 12, 13, 20, 22


def shift(step):
    return [
        (z * 2 + c, ((z + step) % CHIPS) * 2 + c) for z in range(CHIPS) for c in range(2)
    ]


SWAP = [(i, i ^ 1) for i in range(2 * CHIPS)]
SPLIT = [
    (z * 2 + c, ((z + (1 if c == 0 else -1)) % CHIPS) * 2 + c)
    for z in range(CHIPS)
    for c in range(2)
]


def per_device(tokens, inner, outer, down, up, pattern):
    seq = lax.axis_index("seq").astype(jnp.int32)
    core = seq % 2
    mine = lax.dynamic_slice_in_dim(pattern, seq * LOCAL_BLOCKS, LOCAL_BLOCKS, 0).reshape(-1)
    info = jnp.concatenate([seq[None], mine]).astype(jnp.int32)

    def swap(value):
        return lax.ppermute(value, "seq", SWAP)

    def hop(forward, backward):
        return (
            lax.ppermute(forward, "seq", shift(1)),
            lax.ppermute(backward, "seq", shift(-1)),
        )

    partner = swap(tokens)
    forward, backward = hop(tokens, tokens)
    weights = prepare_weights(inner, outer, down, up)
    kv, q, gx = gather_step(0, info, (tokens, partner), weights, None, 0, 0, 1, "query", ())
    own_kv = None
    own0 = 0
    for step in range(1, CHIPS // 2):
        if own_kv is None:
            forward, backward, kv, gx, late = lax.optimization_barrier(
                (forward, backward, kv, gx, info)
            )
            own_query_weights, own_kv_weights = own_head_weights(late, inner, outer, up, weights[2])
        else:
            forward, backward, kv, gx, own_kv = lax.optimization_barrier(
                (forward, backward, kv, gx, own_kv)
            )
        pieces = (forward, backward, swap(forward), swap(backward))
        tiles = 1
        if step == 1:
            edge = jnp.where(core == 0, pieces[2][2 * BLK :], pieces[3][:BLK])
        if step == 2:
            tiles = 2
            pieces += (partner, tokens, edge)
        if step < CHIPS // 2 - 1:
            forward, backward = hop(forward, backward)
        else:
            far = lax.ppermute(jnp.where(core == 0, forward, backward), "seq", SPLIT)
        previous = [(kv, 0)] + ([(own_kv, 1)] if own_kv is not None else []) + [(gx, 2)]
        row0 = {1: 4, 2: 8, 3: 16}[step] * BLK
        kv, own_kv, gx = gather_step(
            step, info, pieces, weights, own_kv_weights, row0, own0, tiles, "both", previous
        )
        own0 += len(pieces[:6]) * SHARD
    far, kv, own_kv, gx = lax.optimization_barrier((far, kv, own_kv, gx))
    far_pieces = (far, swap(far))
    head, gx = attend_global(
        info, far_pieces, own_kv_weights, weights[2], own_kv, gx, own_query_weights
    )
    def far_blocks(mode, kv):
        (kv,) = gather_step(
            CHIPS // 2,
            info,
            far_pieces,
            weights,
            None,
            20 * BLK,
            0,
            1,
            mode,
            [(kv, 0), (gx, None)],
        )
        return kv

    sent = lax.ppermute(head, "seq", [(i + 1, i) for i in range(0, 2 * CHIPS, 2)])
    gx, head = lax.optimization_barrier((gx, head))
    kv = far_blocks("keys", kv)
    sent, kv = lax.optimization_barrier((sent, kv))
    head = jnp.concatenate([head, sent], axis=1)
    sent = lax.ppermute(head, "seq", [(i + 2, i) for i in range(0, 2 * CHIPS, 4)])
    kv, head = lax.optimization_barrier((kv, head))
    kv = far_blocks("values", kv)
    sent, kv = lax.optimization_barrier((sent, kv))
    head = jnp.concatenate([head, sent], axis=1)
    heads = [head] + [
        lax.ppermute(head, "seq", [(i, 0)]) for i in range(4, 2 * CHIPS, 4)
    ]
    rows = attend_local(0, WIDTH, info, q, kv)
    return merge(info, heads, [rows])


def solution(mesh):
    return jax.shard_map(
        per_device,
        mesh=mesh,
        in_specs=(P(("dp", "seq"), None), P(), P(), P(), P(), P("dp", None)),
        out_specs=P(("dp", "seq"), None),
        check_vma=False,
    )
```

```python
import functools

import jax
import jax.numpy as jnp
from jax import lax
from jax.experimental import pallas as pl
from jax.experimental.pallas import tpu as pltpu
from jax.sharding import PartitionSpec as P


HEADS = 32
HD = 128
BLK = 64
RAND = 3
GLOB_BLOCKS = 2
WIDTH = 4096
MB = 64
RANK = 16
TILE = 256
GTILE = 384
GROUP_IN = 8
GROUP_OUT = 4
PAIRS = MB // 2
CHIPS = 8
LOCAL_BLOCKS = 3
SHARD = LOCAL_BLOCKS * BLK
DOC = 3072
PITCH = 72
GLOBAL_ROWS = GLOB_BLOCKS * BLK
OWN_COLS = WIDTH // (2 * CHIPS)
KV_ROWS = 1536


def project_tile(first, count, low_of, x_of, w_in, w_out, mid, out_v):
    low = low_of()
    group_in = GROUP_IN * (2 if count == 1 else 1)
    group_out = GROUP_OUT * (2 if count == 1 else 1)

    def inner_step(i, carry):
        made = []
        for n in range(group_in):
            g = i * group_in + n
            xg = x_of(pl.ds(pl.multiple_of(g * 128, 128), 128))
            for p in range(count):
                part = lax.dot_general(
                    w_in[first + p, g],
                    xg,
                    (((1,), (1,)), ((), ())),
                    preferred_element_type=jnp.float32,
                )
                made.append((g, p, part))
        for g, p, part in made:
            for a in range(2):
                start = pl.multiple_of((p * MB + 2 * g + a) * PITCH, 8)
                for lanes in range(TILE // 128):
                    mid[lanes, pl.ds(start, MB), :] = part[
                        a * MB : (a + 1) * MB, lanes * 128 : (lanes + 1) * 128
                    ]
        return carry

    lax.fori_loop(0, PAIRS // group_in, inner_step, 0)

    def outer_step(i, carry):
        units = [(i * group_out + n, p) for n in range(group_out) for p in range(count)]
        stacks = []
        for h, p in units:
            base = p * MB * PITCH + 2 * h
            parts = []
            for lanes in range(TILE // 128):
                one = mid[lanes, pl.ds(base, MB, stride=PITCH), :]
                two = mid[lanes, pl.ds(base + 1, MB, stride=PITCH), :]
                parts.append(
                    jnp.concatenate([one.astype(jnp.bfloat16), two.astype(jnp.bfloat16)], axis=0)
                )
            stacks.append(
                jnp.concatenate(
                    [jnp.concatenate(parts, axis=1), low[p * RANK : (p + 1) * RANK]], axis=0
                )
            )
        made = [
            lax.dot_general(
                stack,
                w_out[first + p, h],
                (((0,), (0,)), ((), ())),
                preferred_element_type=jnp.float32,
            )
            for stack, (h, p) in zip(stacks, units)
        ]
        for done, (h, p) in zip(made, units):
            out_v[p, :, pl.ds(pl.multiple_of(h * 128, 128), 128)] = done.astype(jnp.bfloat16)
        return carry

    lax.fori_loop(0, HEADS // group_out, outer_step, 0)


def named_block(info, source):
    block = jnp.int32(0)
    for r in range(LOCAL_BLOCKS * RAND):
        named = info[1 + r]
        block = jnp.where(lax.div(named, LOCAL_BLOCKS) == source, lax.rem(named, LOCAL_BLOCKS), block)
    return block


def source_of(info, offset):
    dz, cls = offset
    chip = lax.rem(lax.div(info[0], 2) + (dz + CHIPS), CHIPS)
    return chip * 2 + lax.rem(info[0] + cls, 2)


def step_rows(info, kind):
    core = lax.rem(info[0], 2)
    if kind == 0:
        near = SHARD + jnp.where(core == 0, 0, 2 * BLK)
        glob = jnp.where(info[0] == 0, 0, jnp.where(info[0] == 1, SHARD, -1))
        return [0, BLK, 2 * BLK, near], glob
    if kind == CHIPS // 2:
        offsets = [(kind, 0), (kind, 1)]
    else:
        offsets = [(-kind, 0), (kind, 0), (-kind, 1), (kind, 1)]
    starts = []
    glob = jnp.int32(-1)
    for n, offset in enumerate(offsets):
        source = source_of(info, offset)
        starts.append(n * SHARD + BLK * named_block(info, source))
        glob = jnp.where(source == 0, n * SHARD, glob)
    if kind == 2:
        partner = info[0] + 1 - 2 * core
        starts += [4 * SHARD + BLK * named_block(info, partner), 6 * SHARD, 0, 0]
    return starts, glob


def own_query(x, own_in, own_out, w_down):
    inner = jnp.dot(x, own_in[...], preferred_element_type=jnp.float32)
    low = lax.dot_general(
        x, w_down[0:RANK, :], (((1,), (1,)), ((), ())), preferred_element_type=jnp.float32
    )
    main = jnp.dot(
        inner.astype(jnp.bfloat16), own_out[0:OWN_COLS, :], preferred_element_type=jnp.float32
    )
    lifted = jnp.dot(
        low.astype(jnp.bfloat16), own_out[OWN_COLS:, :], preferred_element_type=jnp.float32
    )
    return (main + lifted).astype(jnp.bfloat16)


def own_keys_values(x_v, span, own_in, own_out):
    quarter = WIDTH // 4
    parts, low = [], None
    for n in range(4):
        cols = slice(n * quarter, (n + 1) * quarter)
        part = jnp.dot(x_v[span, cols], own_in[cols, :], preferred_element_type=jnp.float32)
        parts.append(part[:, 0:128].astype(jnp.bfloat16))
        low = part[:, 128:256] if low is None else low + part[:, 128:256]
    parts.append(low.astype(jnp.bfloat16))
    inner = jnp.concatenate(parts, axis=1)
    return jnp.dot(inner, own_out[...], preferred_element_type=jnp.float32).astype(jnp.bfloat16)


def step_body(kind, pieces, tiles, mode, row0, own0, alias, info, *refs):
    x_hbm = refs[: len(pieces)]
    at = len(pieces)
    with_own, carried = mode == "both", mode in ("keys", "values")
    w_in, w_out, w_down = refs[at : at + 3]
    at += 3
    if with_own:
        own_in, own_out = refs[at : at + 2]
        at += 2
    gx_in = refs[at + alias - 1] if alias else None
    at += alias
    kv_hbm = refs[at]
    at += 1
    if with_own:
        own_hbm = refs[at]
        at += 1
    if mode == "query":
        q_hbm = refs[at]
        at += 1
    if not carried:
        gx_hbm = refs[at]
        at += 1
    x_v, slots_v, mid, out_v, own_v, in_sem, out_sem, own_sem, gx_sem = refs[at:]
    rows = sum(pieces) // GTILE * GTILE
    first, count = PROJECTIONS[mode]
    starts, glob = step_rows(info, kind)

    if carried:
        copies = [
            pltpu.make_async_copy(
                x_hbm[n].at[pl.ds(pl.multiple_of(starts[n] - n * SHARD, BLK), BLK), :],
                slots_v.at[pl.ds(n * BLK, BLK), :],
                in_sem.at[n],
            )
            for n in range(len(pieces))
        ]
        copies.append(
            pltpu.make_async_copy(
                gx_in,
                slots_v.at[pl.ds(len(pieces) * BLK, GLOBAL_ROWS), :],
                in_sem.at[len(pieces)],
            )
        )
    else:
        copies = [
            pltpu.make_async_copy(
                x_hbm[n], x_v.at[pl.ds(n * SHARD, pieces[n]), :], in_sem.at[n]
            )
            for n in range(len(pieces))
        ]
    for copy in copies:
        copy.start()
    for copy in copies:
        copy.wait()

    if not carried:
        gx_copy = pltpu.make_async_copy(
            x_v.at[pl.ds(pl.multiple_of(jnp.maximum(glob, 0), BLK), GLOBAL_ROWS), :],
            gx_hbm,
            gx_sem,
        )

        @pl.when(glob >= 0)
        def _():
            gx_copy.start()

    out_copies = []
    for tile in range(tiles):
        for n in range(0 if carried else TILE // BLK):
            start = pl.multiple_of(starts[4 * tile + n], BLK)

            def move(c, carry, n=n, start=start):
                cols = pl.ds(pl.multiple_of(c * 512, 512), 512)
                slots_v[n * BLK : (n + 1) * BLK, cols] = x_v[pl.ds(start, BLK), cols]
                return carry

            lax.fori_loop(0, WIDTH // 512, move, 0)

        def low_of():
            return lax.dot_general(
                w_down[pl.ds(first * RANK, count * RANK), :],
                slots_v[...],
                (((1,), (1,)), ((), ())),
                preferred_element_type=jnp.float32,
            ).astype(jnp.bfloat16)

        project_tile(
            first, count, low_of, lambda cols: slots_v[:, cols], w_in, w_out, mid, out_v.at[tile]
        )
        for p in range(count):
            if first + p == 0:
                src, dst = out_v.at[tile, p, pl.ds(0, SHARD), :], q_hbm
            else:
                src = out_v.at[tile, p]
                dst = kv_hbm.at[first + p - 1, pl.ds(row0 + tile * TILE, TILE), :]
            copy = pltpu.make_async_copy(src, dst, out_sem.at[tile, p])
            copy.start()
            out_copies.append(copy)

    if with_own:

        def own_step(i, carry):
            span = pl.ds(pl.multiple_of(i * GTILE, GTILE), GTILE)
            own_v[span, :] = own_keys_values(x_v, span, own_in, own_out)
            return carry

        lax.fori_loop(0, rows // GTILE, own_step, 0)
        own_copy = pltpu.make_async_copy(own_v, own_hbm.at[pl.ds(own0, rows), :], own_sem)
        own_copy.start()
        own_copy.wait()
    for copy in out_copies:
        copy.wait()
    if not carried:

        @pl.when(glob >= 0)
        def _():
            gx_copy.wait()


PROJECTIONS = {"query": (0, 3), "both": (1, 2), "keys": (1, 1), "values": (2, 1)}


def gather_step(kind, info, pieces, weights, own_weights, row0, own0, tiles, mode, previous):
    count = len(pieces)
    sizes = tuple(piece.shape[0] for piece in pieces)
    rows = sum(sizes) // GTILE * GTILE
    any_spec = pl.BlockSpec(memory_space=pl.ANY)
    vmem = pl.BlockSpec(memory_space=pltpu.VMEM)
    operands = list(pieces) + list(weights) + (list(own_weights) if mode == "both" else [])
    in_specs = [any_spec] * count + [vmem] * (len(operands) - count)
    out_shape = [jax.ShapeDtypeStruct((2, KV_ROWS, WIDTH), jnp.bfloat16)]
    if mode == "both":
        out_shape.append(jax.ShapeDtypeStruct((DOC, 2 * OWN_COLS), jnp.bfloat16))
    if mode == "query":
        out_shape.append(jax.ShapeDtypeStruct((SHARD, WIDTH), jnp.bfloat16))
    if mode in ("query", "both"):
        out_shape.append(jax.ShapeDtypeStruct((GLOBAL_ROWS, WIDTH), jnp.bfloat16))
    aliases = {}
    for value, out in previous:
        if out is not None:
            aliases[1 + len(operands)] = out
        operands.append(value)
        in_specs.append(any_spec)
    projections = PROJECTIONS[mode][1]
    own_rows = rows if mode == "both" else 16
    return pl.pallas_call(
        functools.partial(step_body, kind, sizes, tiles, mode, row0, own0, len(previous)),
        out_shape=tuple(out_shape),
        grid_spec=pltpu.PrefetchScalarGridSpec(
            num_scalar_prefetch=1,
            grid=(),
            in_specs=in_specs,
            out_specs=(any_spec,) * len(out_shape),
            scratch_shapes=[
                pltpu.VMEM((sum(sizes) if mode in ("query", "both") else BLK, WIDTH), jnp.bfloat16),
                pltpu.VMEM((TILE, WIDTH), jnp.bfloat16),
                pltpu.VMEM((TILE // 128, projections * MB * PITCH, 128), jnp.float32),
                pltpu.VMEM((tiles, projections, TILE, WIDTH), jnp.bfloat16),
                pltpu.VMEM((own_rows, 2 * OWN_COLS), jnp.bfloat16),
                pltpu.SemaphoreType.DMA((count + 1,)),
                pltpu.SemaphoreType.DMA((tiles, projections)),
                pltpu.SemaphoreType.DMA(()),
                pltpu.SemaphoreType.DMA(()),
            ],
        ),
        input_output_aliases=aliases,
        compiler_params=pltpu.CompilerParams(vmem_limit_bytes=46 * 1024 * 1024),
        cost_estimate=pl.CostEstimate(
            flops=tiles * projections * 4 * 10**9, bytes_accessed=20 * 10**6, transcendentals=0
        ),
        name="gather_step",
    )(info, *operands)


KEY_SLOTS = GLOB_BLOCKS + 2 + LOCAL_BLOCKS + LOCAL_BLOCKS * RAND
WINDOW_ROW = GLOB_BLOCKS * BLK
RANDOM_ROW = WINDOW_ROW + (LOCAL_BLOCKS + 2) * BLK
SIDE_COLS = 512
EXP_SCALE = float(HD) ** -0.5 * 1.4426950408889634


def softmax_mix(queries, keys, values, biases):
    scores = []
    for q, k, bias in zip(queries, keys, biases):
        score = lax.dot_general(
            q, k(), (((1,), (1,)), ((), ())), preferred_element_type=jnp.float32
        )
        scores.append(score if bias is None else score + bias)
    peaks = [jnp.max(score, axis=-1, keepdims=True) * EXP_SCALE for score in scores]
    weights = [jnp.exp2(score * EXP_SCALE - peak) for score, peak in zip(scores, peaks)]
    totals = [jnp.sum(weight, axis=-1, keepdims=True) for weight in weights]
    numers = [
        jnp.dot(weight.astype(jnp.bfloat16), v(), preferred_element_type=jnp.float32)
        for weight, v in zip(weights, values)
    ]
    return [
        (numer * (1.0 / total)).astype(jnp.bfloat16) for numer, total in zip(numers, totals)
    ]


def random_block(info, r):
    named, seq = info[1 + r], info[0]
    source = lax.div(named, LOCAL_BLOCKS)
    distance = lax.rem(lax.div(source, 2) - lax.div(seq, 2) + CHIPS, CHIPS)
    other = lax.rem(source + seq, 2)
    ahead = jnp.where(distance < CHIPS // 2, 1, 0)
    step = jnp.where(ahead == 1, distance, CHIPS - distance)
    place = 4 * step + jnp.where(step == 3, 4, 0) + 2 * other + ahead
    place = jnp.where(step == CHIPS // 2, FAR_SLOT + other, place)
    place = jnp.where(distance == 0, PARTNER_SLOT, place)
    return jnp.where(source == seq, lax.rem(named, LOCAL_BLOCKS), place)


def local_body(col0, width, info, q_hbm, kv_hbm, out_ref, q_v, held, sem):
    core = lax.rem(info[0], 2)
    below = jnp.where(core == 0, EDGE_FAR, EDGE_NEAR)
    above = jnp.where(core == 0, EDGE_NEAR, EDGE_FAR)
    runs = [(GLOBAL_SLOT, 0, 2), (below, 2, 1), (0, 3, LOCAL_BLOCKS), (above, 6, 1)]
    runs += [(random_block(info, r), 7 + r, 1) for r in range(LOCAL_BLOCKS * RAND)]
    half = SIDE_COLS
    sides = width // half
    q_copy = pltpu.make_async_copy(q_hbm.at[:, pl.ds(col0, width)], q_v, sem.at[sides, 0])
    q_copy.start()
    copies = []
    for side in range(sides):
        cols = pl.ds(col0 + side * half, half)
        for n, (source, target, count) in enumerate(runs):
            rows = pl.ds(pl.multiple_of(source * BLK, BLK), count * BLK)
            copies.append(
                pltpu.make_async_copy(
                    kv_hbm.at[:, rows, cols],
                    held.at[side, :, pl.ds(target * BLK, count * BLK), :],
                    sem.at[side, n],
                )
            )
    for copy in copies:
        copy.start()
    lane = lax.broadcasted_iota(jnp.int32, (1, 8 * BLK), 1)
    biases = []
    for b in range(LOCAL_BLOCKS):
        block = info[0] * LOCAL_BLOCKS + b
        blocked = ((lane >= 128) & (lane < 192) & (block - 1 < GLOB_BLOCKS)) | (
            (lane >= 256) & (lane < 320) & (block + 1 >= DOC // BLK)
        )
        biases.append(jnp.where(blocked, -jnp.inf, 0.0))
    q_copy.wait()
    for side in range(sides):
        for copy in copies[side * len(runs) : (side + 1) * len(runs)]:
            copy.wait()
        units = [(h, b) for h in range(half // HD) for b in range(LOCAL_BLOCKS)]

        def block_rows(plane, h, b, side=side):
            cols = slice(h * HD, (h + 1) * HD)
            first = WINDOW_ROW + b * BLK
            second = RANDOM_ROW + b * RAND * BLK
            return jnp.concatenate(
                [
                    held[side, plane, 0:WINDOW_ROW, cols],
                    held[side, plane, first : first + 3 * BLK, cols],
                    held[side, plane, second : second + RAND * BLK, cols],
                ],
                axis=0,
            )

        def places(h, b, side=side):
            return slice(b * BLK, (b + 1) * BLK), slice(
                side * half + h * HD, side * half + (h + 1) * HD
            )

        mixed = softmax_mix(
            [q_v[places(h, b)] for h, b in units],
            [functools.partial(block_rows, 0, h, b) for h, b in units],
            [functools.partial(block_rows, 1, h, b) for h, b in units],
            [biases[b] for _, b in units],
        )
        for (h, b), rows in zip(units, mixed):
            out_ref[places(h, b)] = rows


def attend_local(col0, width, info, q, kv):
    any_spec = pl.BlockSpec(memory_space=pl.ANY)
    sides = width // SIDE_COLS
    return pl.pallas_call(
        functools.partial(local_body, col0, width),
        out_shape=jax.ShapeDtypeStruct((SHARD, width), jnp.bfloat16),
        in_specs=[pl.BlockSpec(memory_space=pltpu.SMEM), any_spec, any_spec],
        out_specs=pl.BlockSpec(memory_space=pltpu.VMEM),
        scratch_shapes=[
            pltpu.VMEM((SHARD, width), jnp.bfloat16),
            pltpu.VMEM((sides, 2, KEY_SLOTS * BLK, SIDE_COLS), jnp.bfloat16),
            pltpu.SemaphoreType.DMA((sides + 1, 4 + LOCAL_BLOCKS * RAND)),
        ],
        compiler_params=pltpu.CompilerParams(vmem_limit_bytes=48 * 1024 * 1024),
        cost_estimate=pl.CostEstimate(
            flops=4 * 10**6 * width, bytes_accessed=5 * 10**3 * width, transcendentals=800 * width
        ),
        name="attend_local",
    )(info, q, kv)


def global_body(
    info, x0, x1, own_in, own_out, w_down, own_hbm, gx_old, q_in_hbm, q_out_hbm,
    out_ref, gx_hbm, x_v, kv_v, gx_v, q_in, q_out, sem,
):
    _, glob = step_rows(info, CHIPS // 2)
    known = DOC - GTILE
    x_copies = [
        pltpu.make_async_copy(x, x_v.at[pl.ds(n * SHARD, SHARD), :], sem.at[n])
        for n, x in enumerate((x0, x1))
    ]
    copies = [
        pltpu.make_async_copy(q_in_hbm, q_in, sem.at[2]),
        pltpu.make_async_copy(q_out_hbm, q_out, sem.at[3]),
        pltpu.make_async_copy(own_hbm.at[pl.ds(0, known), :], kv_v.at[pl.ds(0, known), :], sem.at[4]),
    ]
    old_copy = pltpu.make_async_copy(gx_old, gx_v, sem.at[5])
    new_copy = pltpu.make_async_copy(
        x_v.at[pl.ds(pl.multiple_of(jnp.maximum(glob, 0), BLK), GLOBAL_ROWS), :], gx_v, sem.at[5]
    )
    for copy in x_copies:
        copy.start()

    @pl.when(glob < 0)
    def _():
        old_copy.start()

    for copy in copies:
        copy.start()
    for copy in x_copies:
        copy.wait()

    @pl.when(glob >= 0)
    def _():
        new_copy.start()
        new_copy.wait()

    @pl.when(glob < 0)
    def _():
        old_copy.wait()

    gx_copy = pltpu.make_async_copy(gx_v, gx_hbm, sem.at[6])
    gx_copy.start()
    kv_v[pl.ds(known, GTILE), :] = own_keys_values(x_v, slice(0, GTILE), own_in, own_out)
    for copy in copies:
        copy.wait()
    q = own_query(gx_v[...], q_in, q_out, w_down)
    heads = [slice(h * HD, (h + 1) * HD) for h in range(OWN_COLS // HD)]
    mixed = softmax_mix(
        [q[:, cols] for cols in heads],
        [lambda cols=cols: kv_v[:, cols] for cols in heads],
        [lambda cols=cols: kv_v[:, cols.start + OWN_COLS : cols.stop + OWN_COLS] for cols in heads],
        [None] * len(heads),
    )
    for cols, rows in zip(heads, mixed):
        out_ref[:, cols] = rows
    gx_copy.wait()


def attend_global(info, pieces, own_weights, w_down, own_kv, gx, own_query_weights):
    any_spec = pl.BlockSpec(memory_space=pl.ANY)
    vmem = pl.BlockSpec(memory_space=pltpu.VMEM)
    return pl.pallas_call(
        global_body,
        out_shape=(
            jax.ShapeDtypeStruct((GLOBAL_ROWS, OWN_COLS), jnp.bfloat16),
            jax.ShapeDtypeStruct(gx.shape, gx.dtype),
        ),
        in_specs=[pl.BlockSpec(memory_space=pltpu.SMEM), any_spec, any_spec]
        + [vmem] * 3
        + [any_spec] * 4,
        out_specs=(vmem, any_spec),
        scratch_shapes=[
            pltpu.VMEM((GTILE, WIDTH), jnp.bfloat16),
            pltpu.VMEM((DOC, 2 * OWN_COLS), jnp.bfloat16),
            pltpu.VMEM((GLOBAL_ROWS, WIDTH), jnp.bfloat16),
            pltpu.VMEM((WIDTH, OWN_COLS), jnp.bfloat16),
            pltpu.VMEM((OWN_COLS + RANK, OWN_COLS), jnp.bfloat16),
            pltpu.SemaphoreType.DMA((7,)),
        ],
        compiler_params=pltpu.CompilerParams(vmem_limit_bytes=46 * 1024 * 1024),
        cost_estimate=pl.CostEstimate(
            flops=4 * 10**9, bytes_accessed=12 * 10**6, transcendentals=800000
        ),
        name="attend_global",
    )(info, *pieces, *own_weights, w_down, own_kv, gx, *own_query_weights)


def merge_body(heads, info, *refs):
    out_ref = refs[-1]
    at = 0
    for part in refs[heads:-1]:
        width = part.shape[1]
        out_ref[:, at : at + width] = part[...]
        at += width

    @pl.when(info[0] == 0)
    def _():
        at = 0
        for head in refs[:heads]:
            width = head.shape[1]
            out_ref[0:GLOBAL_ROWS, at : at + width] = head[...]
            at += width


def merge(info, heads, parts):
    return pl.pallas_call(
        functools.partial(merge_body, len(heads)),
        out_shape=jax.ShapeDtypeStruct((SHARD, WIDTH), jnp.bfloat16),
        in_specs=[pl.BlockSpec(memory_space=pltpu.SMEM)]
        + [pl.BlockSpec(memory_space=pltpu.VMEM)] * (len(heads) + len(parts)),
        out_specs=pl.BlockSpec(memory_space=pltpu.VMEM),
        compiler_params=pltpu.CompilerParams(vmem_limit_bytes=40 * 1024 * 1024),
        name="merge",
    )(info, *heads, *parts)


def main_body(inner, outer, up, w_in, w_out):
    row = lax.broadcasted_iota(jnp.int32, (MB, MB), 0)
    col = lax.broadcasted_iota(jnp.int32, (MB, MB), 1)
    unit = jnp.where(row == col, 1.0, 0.0).astype(jnp.bfloat16)
    lane = lax.broadcasted_iota(jnp.int32, (MB, 2 * MB), 1)
    zero = jnp.zeros((MB, MB), jnp.bfloat16)

    def pair(n, carry):
        p, g = n // PAIRS, n % PAIRS
        blocks = jnp.concatenate([inner[p, 2 * g], inner[p, 2 * g + 1]], axis=0)
        turned = lax.dot_general(
            unit, blocks, (((1,), (1,)), ((), ())), preferred_element_type=jnp.float32
        )
        w_in[p, g, 0:MB, :] = jnp.where(lane < MB, turned, 0.0).astype(jnp.bfloat16)
        w_in[p, g, MB : 2 * MB, :] = jnp.where(lane < MB, 0.0, turned).astype(jnp.bfloat16)
        w_out[p, g, 0:MB, :] = jnp.concatenate([outer[p, 2 * g], zero], axis=1)
        w_out[p, g, MB : 2 * MB, :] = jnp.concatenate([zero, outer[p, 2 * g + 1]], axis=1)
        cols = pl.ds(pl.multiple_of(g * HD, HD), HD)
        w_out[p, g, 2 * MB : 2 * MB + RANK, :] = up[p, :, cols]
        return carry

    lax.fori_loop(0, 3 * PAIRS, pair, 0, unroll=8)


def prepare_weights(inner, outer, down, up):
    vmem = pl.BlockSpec(memory_space=pltpu.VMEM)
    w_in, w_out = pl.pallas_call(
        main_body,
        out_shape=(
            jax.ShapeDtypeStruct((3, PAIRS, 2 * MB, 2 * MB), jnp.bfloat16),
            jax.ShapeDtypeStruct((3, PAIRS, 2 * MB + RANK, HD), jnp.bfloat16),
        ),
        in_specs=[vmem] * 3,
        out_specs=(vmem, vmem),
        compiler_params=pltpu.CompilerParams(vmem_limit_bytes=40 * 1024 * 1024),
        cost_estimate=pl.CostEstimate(flops=10**9, bytes_accessed=12 * 10**6, transcendentals=0),
        name="main_weights",
    )(inner, outer, up)
    return w_in, w_out, jnp.transpose(down, (0, 2, 1)).reshape(3 * RANK, WIDTH)


def own_body(info, inner, outer, up, w_down, q_in, q_out, kv_in, kv_out):
    own_j = OWN_COLS // MB
    col = lax.broadcasted_iota(jnp.int32, (MB, OWN_COLS), 1)
    row = lax.broadcasted_iota(jnp.int32, (MB, OWN_COLS), 0)
    pick = jnp.where(row == info[0] * own_j + col // MB, 1.0, 0.0).astype(jnp.bfloat16)
    col2 = lax.broadcasted_iota(jnp.int32, (MB, 128), 1)
    row2 = lax.broadcasted_iota(jnp.int32, (MB, 128), 0)
    near = row2 == info[0] * own_j + col2 % own_j
    pick_k = jnp.where(near & (col2 % 8 < own_j), 1.0, 0.0).astype(jnp.bfloat16)
    pick_v = jnp.where(near & (col2 % 8 >= own_j), 1.0, 0.0).astype(jnp.bfloat16)
    unit = jnp.where(
        lax.broadcasted_iota(jnp.int32, (2 * RANK, 128), 0)
        == lax.broadcasted_iota(jnp.int32, (2 * RANK, 128), 1),
        1.0,
        0.0,
    ).astype(jnp.bfloat16)
    own_cols = pl.ds(pl.multiple_of(info[0] * OWN_COLS, OWN_COLS), OWN_COLS)
    span = 512
    wide_col = lax.broadcasted_iota(jnp.int32, (span, OWN_COLS), 1) % MB
    wide_row = lax.broadcasted_iota(jnp.int32, (span, OWN_COLS), 0) // MB
    low_col = lax.broadcasted_iota(jnp.int32, (span, 128), 1) // 8
    low_row = lax.broadcasted_iota(jnp.int32, (span, 128), 0) // MB

    def fill(i, carry):
        rows = pl.ds(pl.multiple_of(i * span, span), span)
        first = i * (span // MB)
        picked = jnp.dot(inner[0, rows, :], pick, preferred_element_type=jnp.float32)
        q_in[rows, :] = jnp.where(wide_col == wide_row + first, picked, 0.0).astype(jnp.bfloat16)
        picked = jnp.dot(inner[1, rows, :], pick_k, preferred_element_type=jnp.float32)
        picked += jnp.dot(inner[2, rows, :], pick_v, preferred_element_type=jnp.float32)
        here = low_col == low_row + first % 16
        kv_in[rows, 0:128] = jnp.where(here, picked, 0.0).astype(jnp.bfloat16)
        turned = lax.dot_general(
            w_down[RANK : 3 * RANK, rows],
            unit,
            (((0,), (0,)), ((), ())),
            preferred_element_type=jnp.float32,
        )
        kv_in[rows, 128:256] = turned.astype(jnp.bfloat16)
        return carry

    lax.fori_loop(0, WIDTH // span, fill, 0)
    q_out[...] = jnp.zeros_like(q_out)
    kv_out[...] = jnp.zeros_like(kv_out)
    tall_row = lax.broadcasted_iota(jnp.int32, (2 * OWN_COLS, MB), 0)
    tall_col = lax.broadcasted_iota(jnp.int32, (2 * OWN_COLS, MB), 1)
    for j in range(own_j):
        q_out[j * MB : (j + 1) * MB, j * MB : (j + 1) * MB] = outer[0, info[0] * own_j + j]
        for p in range(2):
            place = jnp.where(tall_row == tall_col * 8 + (p * own_j + j), 1.0, 0.0)
            at = p * OWN_COLS + j * MB
            kv_out[0 : 2 * OWN_COLS, at : at + MB] = jnp.dot(
                place.astype(jnp.bfloat16),
                outer[1 + p, info[0] * own_j + j],
                preferred_element_type=jnp.float32,
            ).astype(jnp.bfloat16)
    q_out[OWN_COLS : OWN_COLS + RANK, :] = up[0, :, own_cols]
    for p in range(2):
        at = 2 * OWN_COLS + p * RANK
        kv_out[at : at + RANK, p * OWN_COLS : (p + 1) * OWN_COLS] = up[1 + p, :, own_cols]


def own_head_weights(info, inner, outer, up, w_down):
    vmem = pl.BlockSpec(memory_space=pltpu.VMEM)
    shapes = (
        (WIDTH, OWN_COLS),
        (OWN_COLS + RANK, OWN_COLS),
        (WIDTH, 256),
        (2 * OWN_COLS + 128, 2 * OWN_COLS),
    )
    q_in, q_out, kv_in, kv_out = pl.pallas_call(
        own_body,
        out_shape=tuple(jax.ShapeDtypeStruct(shape, jnp.bfloat16) for shape in shapes),
        in_specs=[pl.BlockSpec(memory_space=pltpu.SMEM)] + [vmem] * 4,
        out_specs=(vmem,) * 4,
        compiler_params=pltpu.CompilerParams(vmem_limit_bytes=40 * 1024 * 1024),
        name="own_weights",
    )(info, inner.reshape(3, WIDTH, MB), outer, up, w_down)
    return (q_in, q_out), (kv_in, kv_out)


EDGE_NEAR, PARTNER_SLOT, EDGE_FAR, FAR_SLOT, GLOBAL_SLOT = 3, 12, 13, 20, 22


def shift(step):
    return [
        (z * 2 + c, ((z + step) % CHIPS) * 2 + c) for z in range(CHIPS) for c in range(2)
    ]


SWAP = [(i, i ^ 1) for i in range(2 * CHIPS)]
SPLIT = [
    (z * 2 + c, ((z + (1 if c == 0 else -1)) % CHIPS) * 2 + c)
    for z in range(CHIPS)
    for c in range(2)
]


def per_device(tokens, inner, outer, down, up, pattern):
    seq = lax.axis_index("seq").astype(jnp.int32)
    core = seq % 2
    mine = lax.dynamic_slice_in_dim(pattern, seq * LOCAL_BLOCKS, LOCAL_BLOCKS, 0).reshape(-1)
    info = jnp.concatenate([seq[None], mine]).astype(jnp.int32)

    def swap(value):
        return lax.ppermute(value, "seq", SWAP)

    def hop(forward, backward):
        up = lax.ppermute(forward, "seq", shift(1))
        down = lax.ppermute(backward, "seq", shift(-1))
        return up, down

    partner = swap(tokens)
    forward, backward = hop(tokens, tokens)
    weights = prepare_weights(inner, outer, down, up)
    kv, q, gx = gather_step(0, info, (tokens, partner), weights, None, 0, 0, 1, "query", ())
    own_kv = None
    own0 = 0
    for step in range(1, CHIPS // 2):
        if own_kv is None:
            forward, backward, kv, gx, late = lax.optimization_barrier(
                (forward, backward, kv, gx, info)
            )
            own_query_weights, own_kv_weights = own_head_weights(late, inner, outer, up, weights[2])
        else:
            forward, backward, kv, gx, own_kv = lax.optimization_barrier(
                (forward, backward, kv, gx, own_kv)
            )
        swap_up = swap(forward)
        swap_down = swap(backward)
        pieces = (forward, backward, swap_up, swap_down)
        tiles = 1
        if step == 1:
            edge = jnp.where(core == 0, pieces[2][2 * BLK :], pieces[3][:BLK])
        if step == 2:
            tiles = 2
            pieces += (partner, tokens, edge)
        if step < CHIPS // 2 - 1:
            forward, backward = hop(forward, backward)
        else:
            far = lax.ppermute(jnp.where(core == 0, forward, backward), "seq", SPLIT)
        previous = [(kv, 0)] + ([(own_kv, 1)] if own_kv is not None else []) + [(gx, 2)]
        row0 = {1: 4, 2: 8, 3: 16}[step] * BLK
        kv, own_kv, gx = gather_step(
            step, info, pieces, weights, own_kv_weights, row0, own0, tiles, "both", previous
        )
        own0 += len(pieces[:6]) * SHARD
    far, kv, own_kv, gx = lax.optimization_barrier((far, kv, own_kv, gx))
    far_pieces = (far, swap(far))
    head, gx = attend_global(
        info, far_pieces, own_kv_weights, weights[2], own_kv, gx, own_query_weights
    )

    def far_blocks(mode, kv):
        (kv,) = gather_step(
            CHIPS // 2,
            info,
            far_pieces,
            weights,
            None,
            20 * BLK,
            0,
            1,
            mode,
            [(kv, 0), (gx, None)],
        )
        return kv

    sent = lax.ppermute(head, "seq", [(i + 1, i) for i in range(0, 2 * CHIPS, 2)])
    gx, head = lax.optimization_barrier((gx, head))
    kv = far_blocks("keys", kv)
    sent, kv = lax.optimization_barrier((sent, kv))
    head = jnp.concatenate([head, sent], axis=1)
    sent = lax.ppermute(head, "seq", [(i + 2, i) for i in range(0, 2 * CHIPS, 4)])
    kv, head = lax.optimization_barrier((kv, head))
    kv = far_blocks("values", kv)
    sent, kv = lax.optimization_barrier((sent, kv))
    head = jnp.concatenate([head, sent], axis=1)
    heads = [head] + [
        lax.ppermute(head, "seq", [(i, 0)]) for i in range(4, 2 * CHIPS, 4)
    ]
    rows = attend_local(0, WIDTH, info, q, kv)
    return merge(info, heads, [rows])


def solution(mesh):
    return jax.shard_map(
        per_device,
        mesh=mesh,
        in_specs=(P(("dp", "seq"), None), P(), P(), P(), P(), P("dp", None)),
        out_specs=P(("dp", "seq"), None),
        check_vma=False,
    )
```
